32 devices in a mesh: gx: 2 (over y), gy: 4 (over z), gz: 4 (over x, core).
Axes of the slice: x: 2, y: 2, z: 4, core: 2. Of those that a mesh axis runs over, the one named last changes fastest.
Arguments:
- features: bfloat16 [16, 4, 4, 64, 128], P('gx', 'gy', 'gz'), may hold values from -6 to 6
- positions: bfloat16 [16, 4, 4, 3, 128], P('gx', 'gy', 'gz'), may hold values from 0 to 1
- counts: int32 [16, 4, 4], P('gx', 'gy', 'gz'), may hold values from 1 to 128, as said below
- old_cuts: int32 [3], replicated, may hold values from 0 to 8, as said below
- new_cuts: int32 [3], replicated, may hold values from 0 to 8, as said below
- radial_rates: float32 [2, 2], replicated, may hold values from 0.3 to 3
- conv_weight: bfloat16 [2, 64, 2, 64], replicated, may hold values from -0.5 to 0.5
- up_weight: bfloat16 [2, 256, 64], replicated, may hold values from -0.75 to 0.75
- up_bias: float32 [2, 256], replicated, may hold values from -3 to 3
- down_weight: bfloat16 [2, 64, 256], replicated, may hold values from -0.375 to 0.375
- down_bias: float32 [2, 64], replicated, may hold values from -2 to 2
Outputs:
- moved: bfloat16 [16, 4, 4, 64, 128], P('gx', 'gy', 'gz')
The draws below stay inside these ranges and needn't reach their ends.
Inputs may be any that keep to these rules, and one draw needn't show every extreme that they name: `counts`: some bin of the first x layer holds exactly 128 particles. `old_cuts`: rising from 0 to 8; index k of gx holds the x layers from old_cuts[k] to old_cuts[k+1] - 1, from 2 to 8 of them; with three or more indices along gx one holds exactly 8. `new_cuts`: same form as old_cuts, and each cut differs from the one of old_cuts by -1, 0 or 1.
All inputs are finite; a program needn't handle non-finite values.
Results may differ from the reference program's by a relative error of at most 0.0058.
Values may be sent and summed in bfloat16 or wider, within the bound.
No kernel may reach another device: no remote copies, remote signals or barrier semaphores. Data moves between devices by JAX's collectives and lax.ppermute only.
A program may use at most 128 MiB of HBM per device.

```python
import math
import jax
import jax.numpy as jnp
from jax import lax

F = 64
HID = 256
RADIAL = 2
PSLOT = 128
LAYERS = 2
XL = 4
LCAP = 8
SLOTS = 16
NY = 4
NZ = 4
N_GX = 2


def cut_pair(key):
    base_key = jax.random.fold_in(key, 7)
    key_order, key_pairs, key_moves = jax.random.split(base_key, 3)
    shuffled = jax.random.permutation(key_order, N_GX)
    layer_counts = jnp.full((N_GX,), XL, jnp.int32)
    extra_layers = min(XL, (XL - 2) * (N_GX - 1))
    layer_counts = layer_counts.at[shuffled[0]].add(extra_layers)
    remain = extra_layers
    next_place = 1
    for rank_place in range(1, N_GX):
        taken_layers = min(XL - 2, remain)
        if taken_layers > 0:
            layer_counts = layer_counts.at[shuffled[rank_place]].add(-taken_layers)
            next_place = rank_place + 1
        remain = remain - taken_layers
    pair_count = (N_GX - next_place) // 2
    if pair_count > 0:
        swings = jax.random.randint(key_pairs, (pair_count,), -1, 2).astype(jnp.int32)
        layer_counts = layer_counts.at[shuffled[next_place:next_place + pair_count]].add(swings)
        layer_counts = layer_counts.at[shuffled[next_place + pair_count:next_place + 2 * pair_count]].add(-swings)
    zero_cut = jnp.zeros((1,), jnp.int32)
    old_drawn = jnp.concatenate([zero_cut, jnp.cumsum(layer_counts).astype(jnp.int32)])
    inner_low = layer_counts[:-1]
    inner_high = layer_counts[1:]
    signs = (2 * jax.random.randint(key_moves, (N_GX - 1,), 0, 2) - 1).astype(jnp.int32)
    down_ok = (inner_low >= 3) & (inner_high <= LCAP - 1)
    up_ok = (inner_high >= 3) & (inner_low <= LCAP - 1)
    first_ok = jnp.where(signs < 0, down_ok, up_ok)
    second_ok = jnp.where(signs < 0, up_ok, down_ok)
    cut_moves = jnp.where(first_ok, signs, jnp.where(second_ok, -signs, 0)).astype(jnp.int32)
    odd_cut = jnp.arange(1, N_GX, dtype=jnp.int32) % 2 == 1
    cut_moves = jnp.where(odd_cut, cut_moves, 0).astype(jnp.int32)
    new_drawn = old_drawn + jnp.concatenate([zero_cut, cut_moves, zero_cut])
    return (old_drawn, new_drawn)


def draw_old_cuts(key, part):
    return cut_pair(key)[0]


def draw_new_cuts(key, part):
    return cut_pair(key)[1]


def draw_counts(key, part):
    base_key = jax.random.fold_in(key, 11)
    key_counts, key_y, key_z = jax.random.split(base_key, 3)
    drawn_counts = jax.random.randint(key_counts, (SLOTS, NY, NZ), 1, PSLOT + 1).astype(jnp.int32)
    chosen_y = jax.random.randint(key_y, (), 0, NY)
    chosen_z = jax.random.randint(key_z, (), 0, NZ)
    return drawn_counts.at[0, chosen_y, chosen_z].set(PSLOT)


def levels(rng, extent, cuts, least, high):
    gain = 1.0
    for position, parts in cuts:
        steps = jax.random.uniform(jax.random.fold_in(jax.random.fold_in(rng, 6), position), (parts,), jnp.float32, least / len(cuts), high / len(cuts))
        gain = gain * jnp.repeat(jnp.exp(steps), extent[position] // parts).reshape((-1,) + (1,) * (len(extent) - 1 - position))
    return gain


def bell_draw(rng, dims, width, bound, shards=(), held_as=jnp.bfloat16):
    loudness = levels(rng, dims, shards, -0.22, 0.18) if shards else 1.0
    entries = jax.random.normal(rng, dims, jnp.float32) * width * loudness
    return jnp.minimum(jnp.maximum(entries, -bound), bound).astype(held_as)


def setup_inputs(seed: int = 0) -> dict:
    keys = jax.random.split(jax.random.key(seed), 12)
    features = bell_draw(keys[0], (SLOTS, NY, NZ, F, PSLOT), 1.0, 6.0, ((0, 2), (1, 4), (2, 4)))
    positions = jnp.clip(1.0 * jax.random.uniform(keys[1], (SLOTS, NY, NZ, 3, PSLOT), jnp.float32) ** levels(keys[1], (SLOTS, NY, NZ, 3, PSLOT), ((0, 2), (1, 4), (2, 4)), -0.2, 0.2), 0.0, 1.0).astype(jnp.bfloat16)
    counts = draw_counts(jax.random.fold_in(keys[11], 71), 0)
    old_cuts = draw_old_cuts(jax.random.fold_in(keys[11], 71), 0)
    new_cuts = draw_new_cuts(jax.random.fold_in(keys[11], 71), 0)
    radial_rates = jnp.clip(jnp.exp(jax.random.uniform(keys[5], (LAYERS, RADIAL), jnp.float32, math.log(0.3), math.log(3.0))), 0.3, 3.0)
    conv_weight = bell_draw(keys[6], (LAYERS, F, RADIAL, F), (RADIAL * F) ** -0.5, 0.5)
    up_weight = bell_draw(keys[7], (LAYERS, HID, F), F ** -0.5, 0.75)
    up_bias = bell_draw(keys[8], (LAYERS, HID), 0.5, 3.0, (), jnp.float32)
    down_weight = bell_draw(keys[9], (LAYERS, F, HID), HID ** -0.5, 0.375)
    down_bias = bell_draw(keys[10], (LAYERS, F), 0.3, 2.0, (), jnp.float32)
    return dict(features=features, positions=positions, counts=counts, old_cuts=old_cuts, new_cuts=new_cuts, radial_rates=radial_rates, conv_weight=conv_weight, up_weight=up_weight, up_bias=up_bias, down_weight=down_weight, down_bias=down_bias)


EPSILON = 1e-05

def convolve(features, positions, counts, live_rows, decay_rates, conv_weight, up_weight, up_bias, down_weight, down_bias):
    deep_rows = features.shape[0] - 2
    rows_y = features.shape[1] - 2
    rows_z = features.shape[2] - 2
    feature_count = features.shape[3]
    slot_count = features.shape[4]
    bin_count = deep_rows * rows_y * rows_z
    slot_index = jnp.arange(slot_count, dtype=jnp.int32)
    present = (slot_index < counts[..., None]).astype(jnp.float32)
    centre_positions = positions[1:-1, 1:-1, 1:-1].astype(jnp.float32).reshape(bin_count, 3, slot_count)
    summed = jnp.zeros((bin_count, feature_count, decay_rates.shape[0], slot_count), jnp.float32)
    for step_x in (-1, 0, 1):
        for step_y in (-1, 0, 1):
            for step_z in (-1, 0, 1):
                near_features = features[1 + step_x:1 + step_x + deep_rows, 1 + step_y:1 + step_y + rows_y, 1 + step_z:1 + step_z + rows_z].reshape(bin_count, feature_count, slot_count)
                near_positions = positions[1 + step_x:1 + step_x + deep_rows, 1 + step_y:1 + step_y + rows_y, 1 + step_z:1 + step_z + rows_z].astype(jnp.float32).reshape(bin_count, 3, slot_count)
                near_valid = present[1 + step_x:1 + step_x + deep_rows, 1 + step_y:1 + step_y + rows_y, 1 + step_z:1 + step_z + rows_z].reshape(bin_count, slot_count)
                offset = jnp.array([step_x, step_y, step_z], jnp.float32)
                spread = offset[None, :, None, None] + centre_positions[:, :, :, None] - near_positions[:, :, None, :]
                distance = spread[:, 0] * spread[:, 0] + spread[:, 1] * spread[:, 1] + spread[:, 2] * spread[:, 2]
                kernel = (jnp.exp(-decay_rates[None, :, None, None] * distance[:, None]) * near_valid[:, None, None, :]).astype(jnp.bfloat16)
                summed = summed + jnp.einsum('bfj,bmij->bfmi', near_features.astype(jnp.float32), kernel.astype(jnp.float32))
    gathered = summed.astype(jnp.bfloat16)
    mixed_rows = jnp.einsum('omf,bfmi->boi', conv_weight.astype(jnp.float32), gathered.astype(jnp.float32))
    centred = mixed_rows - lax.optimization_barrier(jnp.mean(mixed_rows, axis=1, keepdims=True))
    normed = (centred * lax.rsqrt(lax.optimization_barrier(jnp.mean(centred * centred, axis=1, keepdims=True)) + EPSILON)).astype(jnp.bfloat16)
    hidden = jax.nn.silu(jnp.einsum('ho,boi->bhi', up_weight.astype(jnp.float32), normed.astype(jnp.float32)) + up_bias[None, :, None]).astype(jnp.bfloat16)
    update = jnp.einsum('oh,bhi->boi', down_weight.astype(jnp.float32), hidden.astype(jnp.float32)) + down_bias[None, :, None]
    centre_features = features[1:-1, 1:-1, 1:-1].reshape(bin_count, feature_count, slot_count).astype(jnp.float32)
    keep_mask = (present[1:-1, 1:-1, 1:-1] * live_rows[:, None, None, None]).reshape(bin_count, 1, slot_count)
    result = ((centre_features + update) * keep_mask).astype(jnp.bfloat16)
    return result.reshape(deep_rows, rows_y, rows_z, feature_count, slot_count)

def to_global(array_in, cuts):
    layer_total = XL * N_GX
    layer_index = jnp.arange(layer_total, dtype=jnp.int32)
    owner_rank = lax.optimization_barrier(jnp.sum((cuts[1:N_GX][None, :] <= layer_index[:, None]).astype(jnp.int32), axis=1)).astype(jnp.int32)
    source = (owner_rank * LCAP + layer_index - cuts[owner_rank]).astype(jnp.int32)
    return jnp.take(array_in, source, axis=0)

def to_slots(array_in, cuts):
    slot_place = jnp.arange(N_GX * LCAP, dtype=jnp.int32)
    owner_rank = slot_place // LCAP
    local_slot = slot_place % LCAP
    layer_index = (cuts[owner_rank] + local_slot).astype(jnp.int32)
    alive_slot = local_slot < cuts[owner_rank + 1] - cuts[owner_rank]
    picked = jnp.take(array_in, jnp.clip(layer_index, 0, XL * N_GX - 1), axis=0)
    return jnp.where(alive_slot[:, None, None, None, None], picked, jnp.zeros_like(picked))

def run_layer(features, positions, counts, decay_rates, conv_weight, up_weight, up_bias, down_weight, down_bias):
    layer_total = features.shape[0]
    padding = ((1, 1), (1, 1), (1, 1), (0, 0), (0, 0))
    padded_features = jnp.pad(features, padding)
    padded_positions = jnp.pad(positions, padding)
    padded_counts = jnp.pad(counts, 1)
    live_rows = jnp.ones((1,), jnp.float32)

    def one_layer(start_row):
        return convolve(lax.dynamic_slice_in_dim(padded_features, start_row, 3, 0), lax.dynamic_slice_in_dim(padded_positions, start_row, 3, 0), lax.dynamic_slice_in_dim(padded_counts, start_row, 3, 0), live_rows, decay_rates, conv_weight, up_weight, up_bias, down_weight, down_bias)[0]
    return lax.map(one_layer, jnp.arange(layer_total, dtype=jnp.int32))

def reference(features, positions, counts, old_cuts, new_cuts, radial_rates, conv_weight, up_weight, up_bias, down_weight, down_bias):
    grid_features = to_global(features, old_cuts)
    grid_positions = to_global(positions, old_cuts)
    grid_counts = to_global(counts, old_cuts)
    first_out = run_layer(grid_features, grid_positions, grid_counts, radial_rates[0], conv_weight[0], up_weight[0], up_bias[0], down_weight[0], down_bias[0])
    second_out = run_layer(first_out, grid_positions, grid_counts, radial_rates[1], conv_weight[1], up_weight[1], up_bias[1], down_weight[1], down_bias[1])
    return to_slots(second_out, new_cuts)
```

```python
import functools
import math

import jax
import jax.numpy as jnp
from jax import lax
from jax.experimental import pallas as pl
from jax.experimental.pallas import tpu as pltpu
from jax.sharding import PartitionSpec as P

EPSILON = 1e-05
FAR = float(2**20)
LOG2E = math.log2(math.e)
HEAD = 8


def shift(block, axis, by):
    count = lax.axis_size(axis)
    return lax.ppermute(block, axis, [(i, (i + by) % count) for i in range(count)])


def partner(block, axis):
    count = lax.axis_size(axis)
    return lax.ppermute(block, axis, [(i, i ^ 1) for i in range(count)])


def across(block, axis):
    count = lax.axis_size(axis)
    pairs = [(i, ((i + 1) ^ 1) - 1) for i in range(1, count - 1)]
    return lax.ppermute(block, axis, pairs + [(0, count - 1), (count - 1, 0)])


def split3(value):
    first = value.astype(jnp.bfloat16).astype(jnp.float32)
    rest = value - first
    second = rest.astype(jnp.bfloat16).astype(jnp.float32)
    third = (rest - second).astype(jnp.bfloat16).astype(jnp.float32)
    return first, second, third


def layer_kernel(
    plan,
    ints,
    flts,
    pos_refs,
    feat_refs,
    conv_ref,
    up_ref,
    upb_ref,
    down_ref,
    downb_ref,
    out_ref,
    gath_ref,
):
    frame_rows, feat_rows, out_rows, features, slots = plan
    start, stop = ints[0], ints[1]
    low, high = ints[2], ints[3]
    feat_at, out_at = ints[4], ints[5]
    row8 = lax.broadcasted_iota(jnp.int32, (8, slots), 0)
    row16 = lax.broadcasted_iota(jnp.int32, (8, 2 * slots), 0)
    chan = lax.broadcasted_iota(jnp.int32, (8, 2 * slots), 1) < slots
    rate = jnp.where(chan, flts[0], flts[1]) * LOG2E
    live3 = row16 < 3
    q1, q2, q3 = split3(jnp.where(live3, -rate, 0.0))

    def one_bin(row, carry):
        at = pos_refs[0][0, row, :, :].astype(jnp.float32)
        at = jnp.concatenate([at, at], axis=1)
        square = jnp.sum(jnp.where(live3, at * at, 0.0), axis=0, keepdims=True)
        terms = jnp.where(live3, 2.0 * rate * at, jnp.where(row16 == 4, -rate * square, 0.0))
        a1, a2, a3 = split3(terms)
        first = jnp.where(row16 == 3, -1.0, a1)
        zero = jnp.zeros_like(a1)
        right = jnp.concatenate(
            [first, a2, a3, a1, a2, q1, q2, q3, q1, q2, q1, zero, zero, zero, zero, zero], axis=0
        )
        right = right.T.astype(jnp.bfloat16)
        total = jnp.zeros((features, 2 * slots), jnp.float32)
        for cz in range(3):
            for cy in range(3):
                lefts = []
                feats = []
                for dx in (-1, 0, 1):
                    near = row + dx
                    inside = jnp.logical_and(near >= low, near < high)
                    gone = jnp.where(inside, flts[8 + 3 * cz + cy], FAR)
                    near = jnp.clip(near, 0, frame_rows - 1)
                    move = jnp.where(
                        row8 == 0,
                        float(dx),
                        jnp.where(
                            row8 == 1,
                            flts[2 + cy],
                            jnp.where(
                                row8 == 2, flts[5 + cz], jnp.where(row8 == 3, -gone, jnp.where(row8 == 4, -1.0, 0.0))
                            ),
                        ),
                    )
                    there = pos_refs[cz][cy, near, :, :].astype(jnp.float32) - move
                    b1 = there.astype(jnp.bfloat16).astype(jnp.float32)
                    b2 = there - b1
                    s1, s2, s3 = split3(there * there)
                    empty = jnp.zeros_like(b1)
                    left = jnp.concatenate(
                        [b1, b1, b1, b2, b2, s1, s1, s1, s2, s2, s3, empty, empty, empty, empty, empty],
                        axis=0,
                    ).astype(jnp.bfloat16)
                    lefts.append(left)
                    source = jnp.clip(near - feat_at, 0, feat_rows - 1)
                    feats.append(feat_refs[cz][cy, source, 0:features, :])
                power = jnp.dot(
                    right, jnp.concatenate(lefts, axis=1), preferred_element_type=jnp.float32
                )
                weight = jnp.exp2(power).astype(jnp.bfloat16)
                total = total + lax.dot_general(
                    jnp.concatenate(feats, axis=1),
                    weight,
                    (((1,), (1,)), ((), ())),
                    preferred_element_type=jnp.float32,
                )
        both = jnp.concatenate([total[:, :slots], total[:, slots:]], axis=0)
        gath_ref[row - out_at] = both.astype(jnp.bfloat16)
        return carry

    lax.fori_loop(start, stop, one_bin, 0)

    for place in range(out_ref.shape[0]):
        row = place + out_at
        live = jnp.logical_and(row >= start, row < stop)

        @pl.when(live)
        def _(place=place, row=row):
            mixed = jnp.dot(conv_ref[...], gath_ref[place], preferred_element_type=jnp.float32)
            centred = mixed - jnp.mean(mixed, axis=0, keepdims=True)
            spread = jnp.mean(centred * centred, axis=0, keepdims=True)
            normed = (centred * lax.rsqrt(spread + EPSILON)).astype(jnp.bfloat16)
            hidden = jnp.dot(up_ref[...], normed, preferred_element_type=jnp.float32) + upb_ref[...]
            hidden = jax.nn.silu(hidden).astype(jnp.bfloat16)
            update = (
                jnp.dot(down_ref[...], hidden, preferred_element_type=jnp.float32) + downb_ref[...]
            )
            source = jnp.clip(row - feat_at, 0, feat_rows - 1)
            centre = feat_refs[0][0, source, 0:features, :].astype(jnp.float32)
            held = pos_refs[0][0, row, :, :].astype(jnp.float32)[3:4, :] == 0.0
            result = jnp.where(held, centre + update, 0.0)
            out_ref[place] = result.astype(jnp.bfloat16)

        @pl.when(jnp.logical_not(live))
        def _(place=place):
            out_ref[place] = jnp.zeros(out_ref.shape[1:], out_ref.dtype)


def run_layer(ints, flts, frames, feats, out_rows, conv, up, upb, down, downb):
    frame_rows = frames[0].shape[1]
    feat_rows = feats[0].shape[1]
    features = up.shape[1]
    slots = frames[0].shape[3]
    plan = (frame_rows, feat_rows, out_rows, features, slots)
    same = feats[0] is frames[0]
    channels = conv.shape[1]
    conv2 = conv.reshape(features, channels * features)

    def body(ints, flts, *refs):
        wide = refs[:3]
        where = [ref.at[:, :, features : features + HEAD, :] for ref in wide]
        if same:
            vals, rest = wide, refs[3:]
        else:
            vals, rest = refs[3:6], refs[6:]
        layer_kernel(plan, ints, flts, where, vals, *rest)

    operands = list(frames) + ([] if same else list(feats))
    operands += [conv2, up, upb[:, None], down, downb[:, None]]
    whole = pl.BlockSpec(memory_space=pltpu.VMEM)
    smem = pl.BlockSpec(memory_space=pltpu.SMEM)
    return pl.pallas_call(
        body,
        out_shape=jax.ShapeDtypeStruct((out_rows, features, slots), jnp.bfloat16),
        in_specs=[smem, smem] + [whole] * len(operands),
        out_specs=whole,
        scratch_shapes=[pltpu.VMEM((out_rows, channels * features, slots), jnp.bfloat16)],
        compiler_params=pltpu.CompilerParams(vmem_limit_bytes=48 * 2**20),
    )(ints, flts, *operands)


def local(
    features,
    positions,
    counts,
    old_cuts,
    new_cuts,
    radial_rates,
    conv_weight,
    up_weight,
    up_bias,
    down_weight,
    down_bias,
):
    peers = lax.axis_size("gx")
    column = lax.axis_index("gx")
    row_y = lax.axis_index("gy")
    row_z = lax.axis_index("gz")
    last_y = lax.axis_size("gy") - 1
    last_z = lax.axis_size("gz") - 1
    slot_rows = features.shape[0]
    width = features.shape[3]
    slots = features.shape[4]
    total = peers * slot_rows // 2
    old_low = old_cuts[column]
    old_high = old_cuts[column + 1]
    new_low = new_cuts[column]
    new_high = new_cuts[column + 1]
    held = old_high - old_low

    lane = jnp.arange(slots, dtype=jnp.int32)
    far = jnp.where(lane < counts[..., None], 0.0, FAR).astype(jnp.bfloat16)
    spare = HEAD - positions.shape[3] - 1
    packed = jnp.concatenate(
        [
            features[:, 0, 0],
            positions[:, 0, 0],
            far[:, 0, 0][:, None, :],
            jnp.zeros((slot_rows, spare, slots), jnp.bfloat16),
        ],
        axis=1,
    )

    if peers == 2:
        most = min(slot_rows, total - 2)
        mine = packed[:most]
        other = lax.ppermute(mine, "gx", [(0, 1), (1, 0)])
        frame_rows = total
        base = jnp.int32(0)
        layer = jnp.arange(total, dtype=jnp.int32)
        cut = old_cuts[1]
        owner = (layer >= cut).astype(jnp.int32)
        place = layer - owner * cut
        source = jnp.where(owner == column, place, most + place)
        frame = jnp.take(jnp.concatenate([mine, other], axis=0), source, axis=0)
        mid_rows = total - 1
        mid_at = column
    else:
        reach = 3
        frame_rows = slot_rows + 4
        base = new_low - 2
        pieces = [packed]
        starts = [old_low]
        for by, rows in ((1, reach), (2, 1)):
            tail_at = jnp.maximum(held - rows, 0)
            tail = lax.dynamic_slice_in_dim(packed, tail_at, rows, 0)
            pieces.append(shift(tail, "gx", by))
            back = jnp.maximum(column - by, 0)
            low, high = old_cuts[back], old_cuts[back + 1]
            starts.append(jnp.maximum(low, high - rows))
            pieces.append(shift(packed[:rows], "gx", -by))
            ahead = jnp.minimum(column + by, peers - 1)
            starts.append(old_cuts[ahead])
        layer = base + jnp.arange(frame_rows, dtype=jnp.int32)
        back1 = jnp.maximum(column - 1, 0)
        ahead1 = jnp.minimum(column + 1, peers - 1)
        first = slot_rows
        at = []
        for piece in pieces:
            at.append(first - slot_rows)
            first += piece.shape[0]
        choice = jnp.where(
            layer >= old_high,
            jnp.where(
                layer >= old_cuts[ahead1 + 1], at[4] + layer - starts[4], at[2] + layer - starts[2]
            ),
            jnp.where(
                layer >= old_low,
                layer - old_low,
                jnp.where(
                    layer >= old_cuts[back1], at[1] + layer - starts[1], at[3] + layer - starts[3]
                ),
            ),
        )
        stacked = jnp.concatenate(pieces, axis=0)
        frame = jnp.take(stacked, jnp.clip(choice, 0, stacked.shape[0] - 1), axis=0)
        mid_rows = slot_rows + 2
        mid_at = jnp.int32(1)

    def spread(block):
        trio = jnp.stack([block, shift(block, "gy", 1), shift(block, "gy", -1)])
        return trio, partner(trio, "gz"), across(trio, "gz")

    odd = row_z % 2
    zero = jnp.float32(0.0)
    far_y = [zero, jnp.where(row_y == 0, FAR, 0.0), jnp.where(row_y == last_y, FAR, 0.0)]
    ends = jnp.logical_or(row_z == 0, row_z == last_z)
    far_z = [zero, zero, jnp.where(ends, FAR, 0.0)]
    step_z = jnp.where(odd == 1, -1.0, 1.0)

    def floats(level):
        gone = [jnp.maximum(far_z[cz], far_y[cy]) for cz in range(3) for cy in range(3)]
        return jnp.stack(
            [
                radial_rates[level, 0],
                radial_rates[level, 1],
                zero,
                jnp.float32(-1.0),
                jnp.float32(1.0),
                zero,
                step_z,
                -step_z,
            ]
            + gone
        )

    low = jnp.int32(0) - base
    high = jnp.int32(total) - base
    mid_start = jnp.maximum(new_low - 1, 0) - base
    mid_stop = jnp.minimum(new_high + 1, total) - base
    zero_int = jnp.int32(0)
    frames = spread(frame)
    first_out = run_layer(
        jnp.stack([mid_start, mid_stop, low, high, zero_int, mid_at]),
        floats(0),
        frames,
        frames,
        mid_rows,
        conv_weight[0],
        up_weight[0],
        up_bias[0],
        down_weight[0],
        down_bias[0],
    )
    feats = spread(first_out)
    second = run_layer(
        jnp.stack([new_low - base, new_high - base, low, high, mid_at, new_low - base]),
        floats(1),
        frames,
        feats,
        slot_rows,
        conv_weight[1],
        up_weight[1],
        up_bias[1],
        down_weight[1],
        down_bias[1],
    )
    return second[:, None, None]


def solution(mesh):
    placed = (P("gx", "gy", "gz", None, None),) * 2 + (P("gx", "gy", "gz"),) + (P(),) * 8
    return jax.shard_map(
        local,
        mesh=mesh,
        in_specs=placed,
        out_specs=P("gx", "gy", "gz", None, None),
        check_vma=False,
    )
```

```python
import functools
import math

import jax
import jax.numpy as jnp
from jax import lax
from jax.experimental import pallas as pl
from jax.experimental.pallas import tpu as pltpu
from jax.sharding import PartitionSpec as P

EPSILON = 1e-05
FAR = float(2**20)
LOG2E = math.log2(math.e)
HEAD = 8


def shift(block, axis, by):
    count = lax.axis_size(axis)
    return lax.ppermute(block, axis, [(i, (i + by) % count) for i in range(count)])


def partner(block, axis):
    count = lax.axis_size(axis)
    return lax.ppermute(block, axis, [(i, i ^ 1) for i in range(count)])


def crossing(block, axis):
    count = lax.axis_size(axis)
    return lax.ppermute(block, axis, [(i, ((i + 1) ^ 1) - 1) for i in range(1, count - 1)])


def split3(value):
    first = value.astype(jnp.bfloat16).astype(jnp.float32)
    rest = value - first
    second = rest.astype(jnp.bfloat16).astype(jnp.float32)
    return first, second, rest - second


def centre_terms(place, row8):
    here = place.astype(jnp.float32)
    live = row8 < 3
    n1, n2, n3 = split3(jnp.sum(jnp.where(live, here * here, 0.0), axis=0, keepdims=True))
    cross = jnp.where(live, -2.0 * here, 0.0)
    ones = jnp.where(live, 1.0, 0.0)
    norm = jnp.where(row8 == 4, n1, jnp.where(row8 == 5, n2, jnp.where(row8 == 6, n3, 0.0)))
    lead = jnp.where(row8 == 3, 1.0, cross + norm)
    stack = jnp.concatenate([lead, cross, cross, ones, ones, ones], axis=0)
    return stack.T.astype(jnp.bfloat16)


def near_terms(place, move):
    there = place.astype(jnp.float32) - move
    pieces = split3(there) + split3(there * there)
    return jnp.concatenate(pieces, axis=0).astype(jnp.bfloat16)


def gather_bins(rows, ints, scales, columns, home, feat_at, row8):
    low, high = ints[2], ints[3]
    sums = []
    for row in rows:
        right = centre_terms(home[row, :, :], row8)
        moves = []
        nears = []
        for dx in (-1, 0, 1):
            near = row + dx
            inside = jnp.logical_and(near >= low, near < high)
            gone = jnp.where(inside, 0.0, FAR)
            moves.append(jnp.where(row8 == 0, float(dx), jnp.where(row8 == 3, -gone, 0.0)))
            nears.append(near)
        items = [(column, dx) for column in columns for dx in range(3)]
        total = None
        for k in range(0, len(items), 2):
            lefts = []
            feats = []
            for (where, vals, base), dx in items[k : k + 2]:
                near = jnp.clip(nears[dx], 0, where.shape[0] - 1)
                lefts.append(near_terms(where[near, :, :], base + moves[dx]))
                source = jnp.clip(near - feat_at, 0, vals.shape[0] - 1)
                feats.append(vals[source, :, :])
            left = lefts[0] if len(lefts) == 1 else jnp.concatenate(lefts, axis=1)
            feat = feats[0] if len(feats) == 1 else jnp.concatenate(feats, axis=1)
            dist = jnp.dot(right, left, preferred_element_type=jnp.float32)
            weight = jnp.concatenate(
                [jnp.exp2(dist * scale).astype(jnp.bfloat16) for scale in scales], axis=0
            )
            part = lax.dot_general(
                feat, weight, (((1,), (1,)), ((), ())), preferred_element_type=jnp.float32
            )
            total = part if total is None else total + part
        sums.append(total)
    return sums


def gather_call(ints, flts, spec, level, home, frames, feats, shape, before, mlp):
    features, slots, head, out_rows, live_rows = shape
    count = len(frames)
    same = feats is None
    channels = 2

    def body(*refs):
        ints, flts = refs[0], refs[1]
        at = 2
        home_ref = refs[at].at[:, features : features + head, :]
        at += 1
        fr = refs[at : at + count]
        at += count
        if same:
            fe = fr
        else:
            fe = refs[at : at + count]
            at += count
        prior = None
        if before is not None:
            prior = refs[at]
            at += 1
        if mlp is not None:
            centre_ref, conv_ref, up_ref, upb_ref, down_ref, downb_ref = refs[at : at + 6]
            at += 6
        out_ref = refs[at]
        row8 = lax.broadcasted_iota(jnp.int32, (head, slots), 0)
        feat_at = ints[4] * (0 if same else 1)
        first = 5 + 2 * level
        start, stop = (ints[0], ints[1]) if level == 0 else (ints[5], ints[6])
        out_at = ints[4] if level == 0 else ints[5]
        scales = [flts[2 * level] * -LOG2E, flts[2 * level + 1] * -LOG2E]
        columns = []
        for index, sub, dy, dz, flags in spec:
            where = fr[index] if sub is None else fr[index].at[sub]
            vals = fe[index] if sub is None else fe[index].at[sub]
            where = where.at[:, features : features + head, :]
            vals = vals.at[:, 0:features, :]
            gone = 0.0
            for flag in flags:
                gone = gone + flts[flag]
            base = jnp.where(row8 == 1, float(dy), 0.0)
            base = jnp.where(row8 == 2, float(dz) * flts[4], base)
            base = jnp.where(row8 == 3, -gone, base)
            base = jnp.where(jnp.logical_and(row8 >= 4, row8 <= 6), -1.0, base)
            columns.append((where, vals, base))

        def step(turn, carry):
            rows = [start + 2 * turn]
            rows.append(jnp.minimum(rows[0] + 1, stop - 1))
            sums = gather_bins(rows, ints, scales, columns, home_ref, feat_at, row8)
            for row, total in zip(rows, sums):
                slot = row - out_at
                if prior is not None:
                    total = total + prior[slot]
                if mlp is None:
                    out_ref[slot] = total
                else:
                    both = jnp.concatenate([total[:, :slots], total[:, slots:]], axis=0)
                    refs[at + 1][slot] = both.astype(jnp.bfloat16)
            return carry

        lax.fori_loop(0, (stop - start + 1) // 2, step, 0)
        if mlp is None:
            return
        gath_ref = refs[at + 1]
        for place in range(0, out_rows, 2):
            group = [p for p in (place, place + 1) if p < live_rows]
            for p in (place, place + 1):
                if p >= live_rows and p < out_rows:
                    out_ref[p] = jnp.zeros((features, slots), jnp.bfloat16)
            if not group:
                continue
            packed = jnp.concatenate([gath_ref[p] for p in group], axis=1)
            mixed = jnp.dot(conv_ref[...], packed, preferred_element_type=jnp.float32)
            centred = mixed - jnp.mean(mixed, axis=0, keepdims=True)
            spread = jnp.mean(centred * centred, axis=0, keepdims=True)
            normed = (centred * lax.rsqrt(spread + EPSILON)).astype(jnp.bfloat16)
            hidden = jnp.dot(up_ref[...], normed, preferred_element_type=jnp.float32)
            hidden = hidden + upb_ref[:, 0 : len(group) * slots]
            half = 0.5 * hidden
            hidden = (half + half * jnp.tanh(half)).astype(jnp.bfloat16)
            update = jnp.dot(down_ref[...], hidden, preferred_element_type=jnp.float32)
            update = update + downb_ref[:, 0 : len(group) * slots]
            for k, p in enumerate(group):
                row = p + out_at
                live = jnp.logical_and(row >= start, row < stop)
                source = jnp.clip(row - feat_at, 0, centre_ref.shape[0] - 1)
                centre = centre_ref[source, 0:features, :].astype(jnp.float32)
                safe = jnp.clip(row, 0, home_ref.shape[0] - 1)
                far = home_ref[safe, :, :].astype(jnp.float32)[3:4, :]
                held = jnp.logical_and(far == 0.0, live)
                result = centre + update[:, k * slots : (k + 1) * slots]
                out_ref[p] = jnp.where(held, result, 0.0).astype(jnp.bfloat16)

    operands = [home] + list(frames) + ([] if same else list(feats))
    if before is not None:
        operands.append(before)
    whole = pl.BlockSpec(memory_space=pltpu.VMEM)
    smem = pl.BlockSpec(memory_space=pltpu.SMEM)
    scratch = []
    if mlp is None:
        out_shape = jax.ShapeDtypeStruct((out_rows, features, channels * slots), jnp.float32)
    else:
        operands += list(mlp)
        out_shape = jax.ShapeDtypeStruct((out_rows, features, slots), jnp.bfloat16)
        scratch = [pltpu.VMEM((out_rows, channels * features, slots), jnp.bfloat16)]
    pairs = live_rows * 3 * len(spec)
    return pl.pallas_call(
        body,
        out_shape=out_shape,
        in_specs=[smem, smem] + [whole] * len(operands),
        out_specs=whole,
        scratch_shapes=scratch,
        cost_estimate=pl.CostEstimate(
            flops=pairs * 2 * slots * slots * (2 * features + 48),
            transcendentals=pairs * 2 * slots * slots,
            bytes_accessed=pairs * 4 * slots * slots,
        ),
        compiler_params=pltpu.CompilerParams(vmem_limit_bytes=32 * 2**20),
    )(ints, flts, *operands)


def local(
    features,
    positions,
    counts,
    old_cuts,
    new_cuts,
    radial_rates,
    conv_weight,
    up_weight,
    up_bias,
    down_weight,
    down_bias,
):
    peers = lax.axis_size("gx")
    column = lax.axis_index("gx")
    row_y = lax.axis_index("gy")
    row_z = lax.axis_index("gz")
    last_y = lax.axis_size("gy") - 1
    last_z = lax.axis_size("gz") - 1
    slot_rows = features.shape[0]
    width = features.shape[3]
    slots = features.shape[4]
    total = peers * slot_rows // 2
    old_low = old_cuts[column]
    old_high = old_cuts[column + 1]
    new_low = new_cuts[column]
    new_high = new_cuts[column + 1]
    held = old_high - old_low

    lane = jnp.arange(slots, dtype=jnp.int32)
    far = jnp.where(lane < counts[..., None], 0.0, FAR).astype(jnp.bfloat16)
    spare = HEAD - positions.shape[3] - 1
    packed = jnp.concatenate(
        [
            features[:, 0, 0],
            positions[:, 0, 0],
            far[:, 0, 0][:, None, :],
            jnp.zeros((slot_rows, spare, slots), jnp.bfloat16),
        ],
        axis=1,
    )

    if peers == 2:
        most = min(slot_rows, total - 2)
        mine = packed[:most]
        other = lax.ppermute(mine, "gx", [(0, 1), (1, 0)])
        frame_rows = total
        base = jnp.int32(0)
        layer = jnp.arange(total, dtype=jnp.int32)
        cut = old_cuts[1]
        owner = (layer >= cut).astype(jnp.int32)
        place = layer - owner * cut
        source = jnp.where(owner == column, place, most + place)
        frame = jnp.take(jnp.concatenate([mine, other], axis=0), source, axis=0)
        mid_rows = total - 1
        mid_at = column
    else:
        reach = 3
        frame_rows = slot_rows + 4
        base = new_low - 2
        pieces = [packed]
        starts = [old_low]
        for by, rows in ((1, reach), (2, 1)):
            tail_at = jnp.maximum(held - rows, 0)
            tail = lax.dynamic_slice_in_dim(packed, tail_at, rows, 0)
            pieces.append(shift(tail, "gx", by))
            back = jnp.maximum(column - by, 0)
            low, high = old_cuts[back], old_cuts[back + 1]
            starts.append(jnp.maximum(low, high - rows))
            pieces.append(shift(packed[:rows], "gx", -by))
            ahead = jnp.minimum(column + by, peers - 1)
            starts.append(old_cuts[ahead])
        layer = base + jnp.arange(frame_rows, dtype=jnp.int32)
        back1 = jnp.maximum(column - 1, 0)
        ahead1 = jnp.minimum(column + 1, peers - 1)
        first = slot_rows
        at = []
        for piece in pieces:
            at.append(first - slot_rows)
            first += piece.shape[0]
        choice = jnp.where(
            layer >= old_high,
            jnp.where(
                layer >= old_cuts[ahead1 + 1], at[4] + layer - starts[4], at[2] + layer - starts[2]
            ),
            jnp.where(
                layer >= old_low,
                layer - old_low,
                jnp.where(
                    layer >= old_cuts[back1], at[1] + layer - starts[1], at[3] + layer - starts[3]
                ),
            ),
        )
        stacked = jnp.concatenate(pieces, axis=0)
        frame = jnp.take(stacked, jnp.clip(choice, 0, stacked.shape[0] - 1), axis=0)
        mid_rows = slot_rows + 2
        mid_at = jnp.int32(1)

    odd = row_z % 2
    ends = jnp.logical_or(row_z == 0, row_z == last_z)
    flts = jnp.concatenate(
        [
            radial_rates.reshape(-1),
            jnp.stack(
                [
                    jnp.where(odd == 1, -1.0, 1.0),
                    jnp.where(row_y == 0, FAR, 0.0),
                    jnp.where(row_y == last_y, FAR, 0.0),
                    jnp.where(ends, FAR, 0.0),
                ]
            ),
        ]
    )
    ints = jnp.stack(
        [
            jnp.maximum(new_low - 1, 0) - base,
            jnp.minimum(new_high + 1, total) - base,
            0 - base,
            total - base,
            mid_at,
            new_low - base,
            new_high - base,
        ]
    )
    up_far, down_far, z_far = 5, 6, 7
    own = [(0, None, 0, 0, ())]
    sides = [
        (0, None, -1, 0, (up_far,)),
        (1, None, 1, 0, (down_far,)),
        (2, 0, 0, 1, ()),
        (2, 1, -1, 1, (up_far,)),
        (2, 2, 1, 1, (down_far,)),
    ]
    cross = [
        (0, 0, 0, -1, (z_far,)),
        (0, 1, -1, -1, (up_far, z_far)),
        (0, 2, 1, -1, (down_far, z_far)),
    ]

    def weights(level):
        conv = conv_weight[level].reshape(width, -1)
        wide = (2 * slots,)
        upb = jnp.broadcast_to(up_bias[level][:, None], up_bias.shape[1:] + wide)
        downb = jnp.broadcast_to(down_bias[level][:, None], down_bias.shape[1:] + wide)
        return (conv, up_weight[level], upb, down_weight[level], downb)

    def layer(level, block, places, out_rows, live_rows):
        shape = (width, slots, HEAD, out_rows, live_rows)
        up = shift(block, "gy", 1)
        down = shift(block, "gy", -1)
        if places is None:
            home, feats1, feats2, feats3 = block, None, None, None
            frames1 = [block]
        else:
            home, up_at, down_at, near_at, far_at = places
            frames1, feats1 = [home], [block]
        first = gather_call(
            ints, flts, own, level, home, frames1, feats1, shape, None, None
        )
        trio = jnp.stack([block, up, down])
        far = crossing(trio, "gz")
        near = partner(trio, "gz")
        if places is None:
            frames2, frames3 = [up, down, near], [far]
        else:
            frames2, feats2 = [up_at, down_at, near_at], [up, down, near]
            frames3, feats3 = [far_at], [far]
        second = gather_call(
            ints, flts, sides, level, home, frames2, feats2, shape, first, None
        )
        out = gather_call(
            ints,
            flts,
            cross,
            level,
            home,
            frames3,
            feats3,
            shape,
            second,
            (block,) + weights(level),
        )
        return out, (block, up, down, near, far)

    mid, places = layer(0, frame, None, mid_rows, mid_rows)
    most = min(slot_rows, total - 2 * (peers - 1))
    second, _ = layer(1, mid, places, slot_rows, most)
    return second[:, None, None]


def solution(mesh):
    placed = (P("gx", "gy", "gz", None, None),) * 2 + (P("gx", "gy", "gz"),) + (P(),) * 8
    return jax.shard_map(
        local,
        mesh=mesh,
        in_specs=placed,
        out_specs=P("gx", "gy", "gz", None, None),
        check_vma=False,
    )
```

```python
import math

import jax
import jax.numpy as jnp
from jax import lax
from jax.experimental import pallas as pl
from jax.experimental.pallas import tpu as pltpu
from jax.sharding import PartitionSpec as P

EPSILON = 1e-05
FAR = float(2**20)
LOG2E = math.log2(math.e)
HEAD = 8
TERMS = 48
VMEM_LIMIT = 32 * 2**20

MID_START, MID_STOP, LOW, HIGH, MID_AT, OUT_START, OUT_STOP, CUT, COLUMN = range(9)
STEP_Z, FAR_UP, FAR_DOWN, FAR_Z = 4, 5, 6, 7


def whole():
    return pl.BlockSpec(memory_space=pltpu.VMEM)


def scalars():
    return pl.BlockSpec(memory_space=pltpu.SMEM)


def params():
    return pltpu.CompilerParams(vmem_limit_bytes=VMEM_LIMIT)


def shift(block, axis, by):
    count = lax.axis_size(axis)
    return lax.ppermute(block, axis, [(i, (i + by) % count) for i in range(count)])


def partner(block, axis):
    count = lax.axis_size(axis)
    return lax.ppermute(block, axis, [(i, i ^ 1) for i in range(count)])


def crossing(block, axis):
    count = lax.axis_size(axis)
    return lax.ppermute(block, axis, [(i, ((i + 1) ^ 1) - 1) for i in range(1, count - 1)])


def split3(value):
    first = value.astype(jnp.bfloat16).astype(jnp.float32)
    rest = value - first
    second = rest.astype(jnp.bfloat16).astype(jnp.float32)
    return first, second, rest - second


def pack(features, positions, counts, old_cuts, new_cuts, rates, rows):
    slot_rows, _, _, width, slots = features.shape
    peers = lax.axis_size("gx")
    last_y = lax.axis_size("gy") - 1
    last_z = lax.axis_size("gz") - 1
    total = peers * slot_rows // 2

    def body(feat_ref, pos_ref, count_ref, old_ref, new_ref, rate_ref, where_ref, out_ref, int_ref, flt_ref, sem):
        copy = pltpu.make_async_copy(
            feat_ref.at[0:rows, 0, 0], out_ref.at[:, 0:width, :], sem
        )
        copy.start()
        column, row_y, row_z = where_ref[0], where_ref[1], where_ref[2]
        new_low, new_high = new_ref[column], new_ref[column + 1]
        if peers == 2:
            base, mid_at = 0, column
        else:
            base, mid_at = new_low - 2, 1
        int_ref[MID_START] = jnp.maximum(new_low - 1, 0) - base
        int_ref[MID_STOP] = jnp.minimum(new_high + 1, total) - base
        int_ref[LOW] = jnp.int32(0) - base
        int_ref[HIGH] = jnp.int32(total) - base
        int_ref[MID_AT] = jnp.int32(mid_at)
        int_ref[OUT_START] = new_low - base
        int_ref[OUT_STOP] = new_high - base
        int_ref[CUT] = old_ref[1]
        int_ref[COLUMN] = column
        for k in range(2):
            for m in range(2):
                flt_ref[2 * k + m] = rate_ref[k, m]
        flt_ref[STEP_Z] = jnp.where(row_z % 2 == 1, -1.0, 1.0)
        flt_ref[FAR_UP] = jnp.where(row_y == 0, FAR, 0.0)
        flt_ref[FAR_DOWN] = jnp.where(row_y == last_y, FAR, 0.0)
        flt_ref[FAR_Z] = jnp.where(jnp.logical_or(row_z == 0, row_z == last_z), FAR, 0.0)
        lane = lax.broadcasted_iota(jnp.int32, (1, slots), 1)
        spare = jnp.zeros((HEAD - 4, slots), jnp.float32)
        for row in range(rows):
            place = [pos_ref[d, row : row + 1, :].astype(jnp.float32) for d in range(3)]
            far = jnp.where(lane < count_ref[row], 0.0, FAR)
            block = jnp.concatenate(place + [far, spare], axis=0)
            out_ref[row, width : width + HEAD, :] = block.astype(jnp.bfloat16)
        copy.wait()

    where = jnp.stack([lax.axis_index("gx"), lax.axis_index("gy"), lax.axis_index("gz")])
    return pl.pallas_call(
        body,
        out_shape=(
            jax.ShapeDtypeStruct((rows, width + HEAD, slots), jnp.bfloat16),
            jax.ShapeDtypeStruct((9,), jnp.int32),
            jax.ShapeDtypeStruct((8,), jnp.float32),
        ),
        in_specs=[pl.BlockSpec(memory_space=pl.ANY), whole()] + [scalars()] * 5,
        out_specs=(whole(), scalars(), scalars()),
        scratch_shapes=[pltpu.SemaphoreType.DMA],
        compiler_params=params(),
    )(
        features,
        jnp.transpose(positions[:, 0, 0], (1, 0, 2)),
        counts.reshape(-1),
        old_cuts,
        new_cuts,
        rates,
        where,
    )


def assemble(ints, mine, other, rows):
    def body(int_ref, mine_ref, other_ref, out_ref):
        cut, column = int_ref[CUT], int_ref[COLUMN]
        for row in range(rows):
            owner = jnp.int32(row) >= cut
            place = jnp.where(owner, row - cut, row)
            place = jnp.clip(place, 0, mine_ref.shape[0] - 1)
            is_mine = owner.astype(jnp.int32) == column

            @pl.when(is_mine)
            def _(row=row, place=place):
                out_ref[row] = mine_ref[place]

            @pl.when(jnp.logical_not(is_mine))
            def _(row=row, place=place):
                out_ref[row] = other_ref[place]

    return pl.pallas_call(
        body,
        out_shape=jax.ShapeDtypeStruct((rows,) + mine.shape[1:], mine.dtype),
        in_specs=[scalars(), whole(), whole()],
        out_specs=whole(),
        compiler_params=params(),
    )(ints, mine, other)


def centre_terms(place, along, row8):
    here = place.astype(jnp.float32)
    live = row8 < 3
    at = jnp.where(row8 == 0, here + along, jnp.where(live, here, 0.0))
    n1, n2, n3 = split3(jnp.sum(at * at, axis=0, keepdims=True))
    minus = jnp.where(live, -2.0 * here, 0.0)
    norm = jnp.where(row8 == 4, n1, jnp.where(row8 == 5, n2, jnp.where(row8 == 6, n3, 0.0)))
    turned = jnp.sum(jnp.where(row8 == 0, minus, 0.0), axis=0, keepdims=True)
    lead = jnp.where(row8 == 3, 1.0, jnp.where(row8 == 7, turned, minus + norm))
    other = jnp.where(jnp.logical_or(row8 == 0, row8 == 3), -2.0 * along, minus)
    ones = jnp.where(live, 1.0, 0.0)
    stack = jnp.concatenate([lead, other, ones, ones, ones, jnp.zeros_like(ones)], axis=0)
    return stack.T.astype(jnp.bfloat16)


def near_terms(place, base, along, gone, row8):
    move = jnp.where(row8 == 3, base - gone, jnp.where(row8 == 7, -along, base))
    there = place.astype(jnp.float32) - move
    first = there.astype(jnp.bfloat16).astype(jnp.float32)
    rest = there - first
    second = jnp.where(row8 == 0, there, jnp.where(row8 == 3, along, rest))
    at = jnp.where(row8 == 0, there + along, jnp.where(row8 < 3, there, 0.0))
    q1, q2, q3 = split3(at * at)
    stack = jnp.concatenate([first, second, q1, q2, q3, jnp.zeros_like(q1)], axis=0)
    return stack.astype(jnp.bfloat16)


def gather_bins(rows, scales, near_ref, feats, right_ref, feat_at):
    sums = []
    for row in rows:
        right = right_ref[row]
        items = [(c, dx) for c in range(len(feats)) for dx in range(3)]
        total = None
        for k in range(0, len(items), 2):
            lefts = []
            vals = []
            for c, dx in items[k : k + 2]:
                lefts.append(near_ref[c, row + dx])
                source = jnp.clip(row + dx - 1 - feat_at, 0, feats[c].shape[0] - 1)
                vals.append(feats[c][source, :, :])
            left = lefts[0] if len(lefts) == 1 else jnp.concatenate(lefts, axis=1)
            feat = vals[0] if len(vals) == 1 else jnp.concatenate(vals, axis=1)
            dist = jnp.dot(right, left, preferred_element_type=jnp.float32)
            weight = jnp.concatenate(
                [jnp.exp2(dist * scale).astype(jnp.bfloat16) for scale in scales], axis=0
            )
            part = lax.dot_general(
                feat, weight, (((1,), (1,)), ((), ())), preferred_element_type=jnp.float32
            )
            total = part if total is None else total + part
        sums.append(total)
    return sums


def views(spec, arrays, start, size):
    found = []
    for index, sub, *_ in spec:
        ref = arrays[index] if sub is None else arrays[index].at[sub]
        found.append(ref.at[:, start : start + size, :])
    return found


def gather_call(stage, level, ints, flts, spec, frame, feats, right, near, before, extra, out_rows):
    frame_rows, tall, slots = frame.shape
    features = tall - HEAD
    centre = frame_rows // 2
    make_right = right is None
    make_near = near is None
    inputs = [frame] + list(feats)
    if not make_right:
        inputs.append(right)
    if not make_near:
        inputs.append(near)
    if before is not None:
        inputs.append(before)
    inputs += list(extra)
    outs = []
    wide = 2 * slots
    if stage < 2:
        outs.append(jax.ShapeDtypeStruct((out_rows, features, wide), jnp.float32))
    else:
        outs.append(jax.ShapeDtypeStruct((out_rows, features, slots), jnp.bfloat16))
    if make_right:
        outs.append(jax.ShapeDtypeStruct((frame_rows, slots, TERMS), jnp.bfloat16))
    if make_near:
        outs.append(
            jax.ShapeDtypeStruct((len(spec), frame_rows + 2, TERMS, slots), jnp.bfloat16)
        )
    if stage == 0:
        hid = extra[0].shape[2]
        outs.append(jax.ShapeDtypeStruct((hid, features), jnp.bfloat16))
        outs.append(jax.ShapeDtypeStruct((hid, wide), jnp.float32))
        outs.append(jax.ShapeDtypeStruct((features, wide), jnp.float32))

    def body(*refs):
        refs = list(refs)
        ints, flts = refs.pop(0), refs.pop(0)
        home = refs.pop(0)
        vals = [refs.pop(0) for _ in feats]
        right_ref = None if make_right else refs.pop(0)
        near_ref = None if make_near else refs.pop(0)
        prior = None if before is None else refs.pop(0)
        extras = [refs.pop(0) for _ in extra]
        out_ref = refs.pop(0)
        right_ref = refs.pop(0) if make_right else right_ref
        near_ref = refs.pop(0) if make_near else near_ref
        start, stop = (
            (ints[MID_START], ints[MID_STOP]) if level == 0 else (ints[OUT_START], ints[OUT_STOP])
        )
        out_at = ints[MID_AT] if level == 0 else ints[OUT_START]
        feat_at = jnp.int32(0) if level == 0 else ints[MID_AT]
        row8 = lax.broadcasted_iota(jnp.int32, (HEAD, slots), 0)
        scales = [flts[2 * level + m] * -LOG2E for m in range(2)]

        if make_right:
            for row in range(frame_rows):
                place = home[row, features:tall, :]
                right_ref[row] = centre_terms(place, float(centre - row), row8)
        if make_near:
            edge = jnp.where(row8 == 3, FAR, 0.0)
            edge = jnp.concatenate([edge] + [jnp.zeros_like(edge)] * (TERMS // HEAD - 1), axis=0)
            edge = edge.astype(jnp.bfloat16)
            wheres = views(spec, vals, features, HEAD)
            for c, (_, _, dy, dz, flags) in enumerate(spec):
                near_ref[c, 0] = edge
                near_ref[c, frame_rows + 1] = edge
                gone = jnp.float32(0.0)
                for flag in flags:
                    gone = gone + flts[flag]
                base = jnp.where(row8 == 1, float(dy), 0.0)
                base = jnp.where(row8 == 2, float(dz) * flts[STEP_Z], base)
                base = jnp.where(jnp.logical_and(row8 >= 4, row8 <= 6), -1.0, base)
                for row in range(frame_rows):
                    inside = jnp.logical_and(row >= ints[LOW], row < ints[HIGH])
                    lost = gone + jnp.where(inside, 0.0, FAR)
                    near_ref[c, row + 1] = near_terms(
                        wheres[c][row, :, :], base, float(centre - row), lost, row8
                    )
        heads = views(spec, vals, 0, features)

        if stage == 0:
            up_ref, upb_ref, downb_ref = extras
            wup_ref, wupb_ref, wdownb_ref = refs[:3]
            wup_ref[...] = up_ref[level].astype(jnp.float32).T.astype(jnp.bfloat16)
            lift = jnp.broadcast_to(upb_ref[level : level + 1, :], (slots, upb_ref.shape[1])).T
            wupb_ref[...] = jnp.concatenate([lift, lift], axis=1)
            low = jnp.broadcast_to(downb_ref[level : level + 1, :], (slots, features))
            low = jnp.concatenate([low, low], axis=1).T[0:features, :]
            wdownb_ref[...] = jnp.concatenate([low, low], axis=1)

        def pair(turn):
            first = start + 2 * turn
            return [first, jnp.minimum(first + 1, stop - 1)]

        turns = (stop - start + 1) // 2
        if stage < 2:

            def step(turn, carry):
                rows = pair(turn)
                sums = gather_bins(rows, scales, near_ref, heads, right_ref, feat_at)
                for row, total in zip(rows, sums):
                    if prior is not None:
                        total = total + prior[row - out_at]
                    out_ref[row - out_at] = total
                return carry

            lax.fori_loop(0, turns, step, 0)
            return

        centre_ref, conv_ref, down_ref, wup_ref, wupb_ref, wdownb_ref = extras
        gath_ref = refs[0]

        def finish(rows, slot):
            mixed = jnp.dot(conv_ref[level], gath_ref[slot], preferred_element_type=jnp.float32)
            centred = mixed - jnp.mean(mixed, axis=0, keepdims=True)
            spread = jnp.mean(centred * centred, axis=0, keepdims=True)
            normed = (centred * lax.rsqrt(spread + EPSILON)).astype(jnp.bfloat16)
            hidden = jnp.dot(wup_ref[...], normed, preferred_element_type=jnp.float32)
            half = 0.5 * (hidden + wupb_ref[...])
            hidden = (half + half * jnp.tanh(half)).astype(jnp.bfloat16)
            update = jnp.dot(down_ref[level], hidden, preferred_element_type=jnp.float32)
            update = update + wdownb_ref[...]
            for k, row in enumerate(rows):
                source = jnp.clip(row - feat_at, 0, centre_ref.shape[0] - 1)
                kept = centre_ref[source, 0:features, :].astype(jnp.float32)
                far = home[row, features:tall, :].astype(jnp.float32)[3:4, :]
                result = kept + update[:, k * slots : (k + 1) * slots]
                out_ref[row - out_at] = jnp.where(far == 0.0, result, 0.0).astype(jnp.bfloat16)

        for place in range(out_rows):
            out_ref[place] = jnp.zeros((features, slots), jnp.bfloat16)

        def step(turn, carry):
            rows = pair(turn)
            sums = gather_bins(rows, scales, near_ref, heads, right_ref, feat_at)
            finish(pair(jnp.maximum(turn - 1, 0)), (turn + 1) % 2)
            both = []
            for row, total in zip(rows, sums):
                total = total + prior[row - out_at]
                both.append(jnp.concatenate([total[:, :slots], total[:, slots:]], axis=0))
            gath_ref[turn % 2] = jnp.concatenate(both, axis=1).astype(jnp.bfloat16)
            return carry

        lax.fori_loop(0, turns, step, 0)
        finish(pair(turns - 1), (turns + 1) % 2)

    pairs = out_rows * 3 * len(spec)
    scratch = [pltpu.VMEM((2, 2 * features, wide), jnp.bfloat16)] if stage == 2 else []
    return pl.pallas_call(
        body,
        out_shape=tuple(outs),
        in_specs=[scalars(), scalars()] + [whole()] * len(inputs),
        out_specs=tuple(whole() for _ in outs),
        scratch_shapes=scratch,
        cost_estimate=pl.CostEstimate(
            flops=pairs * 2 * slots * slots * (2 * features + TERMS),
            transcendentals=pairs * 2 * slots * slots,
            bytes_accessed=pairs * 4 * slots * slots,
        ),
        compiler_params=params(),
    )(ints, flts, *inputs)


def local(
    features,
    positions,
    counts,
    old_cuts,
    new_cuts,
    radial_rates,
    conv_weight,
    up_weight,
    up_bias,
    down_weight,
    down_bias,
):
    peers = lax.axis_size("gx")
    slot_rows = features.shape[0]
    total = peers * slot_rows // 2
    most = min(slot_rows, total - 2 * (peers - 1))
    packed, ints, flts = pack(
        features, positions, counts, old_cuts, new_cuts, radial_rates, most
    )

    if peers == 2:
        other = lax.ppermute(packed, "gx", [(0, 1), (1, 0)])
        frame = assemble(ints, packed, other, total)
        mid_rows = total - 1
    else:
        column = lax.axis_index("gx")
        old_low = old_cuts[column]
        old_high = old_cuts[column + 1]
        held = old_high - old_low
        frame_rows = slot_rows + 4
        base = new_cuts[column] - 2
        pieces = [packed]
        starts = [old_low]
        for by, rows in ((1, 3), (2, 1)):
            tail_at = jnp.maximum(held - rows, 0)
            tail = lax.dynamic_slice_in_dim(packed, tail_at, rows, 0)
            pieces.append(shift(tail, "gx", by))
            back = jnp.maximum(column - by, 0)
            starts.append(jnp.maximum(old_cuts[back], old_cuts[back + 1] - rows))
            pieces.append(shift(packed[:rows], "gx", -by))
            starts.append(old_cuts[jnp.minimum(column + by, peers - 1)])
        layer = base + jnp.arange(frame_rows, dtype=jnp.int32)
        before = old_cuts[jnp.maximum(column - 1, 0)]
        after = old_cuts[jnp.minimum(column + 1, peers - 1) + 1]
        at = []
        first = 0
        for piece, begin in zip(pieces, starts):
            at.append(first + layer - begin)
            first += piece.shape[0]
        choice = jnp.where(
            layer >= old_high,
            jnp.where(layer >= after, at[4], at[2]),
            jnp.where(layer >= old_low, at[0], jnp.where(layer >= before, at[1], at[3])),
        )
        frame = jnp.take(jnp.concatenate(pieces, axis=0), jnp.clip(choice, 0, first - 1), axis=0)
        mid_rows = slot_rows + 2

    own = [(0, None, 0, 0, ())]
    sides = [
        (0, None, -1, 0, (FAR_UP,)),
        (1, None, 1, 0, (FAR_DOWN,)),
        (2, 0, 0, 1, ()),
        (2, 1, -1, 1, (FAR_UP,)),
        (2, 2, 1, 1, (FAR_DOWN,)),
    ]
    cross = [
        (0, 0, 0, -1, (FAR_Z,)),
        (0, 1, -1, -1, (FAR_UP, FAR_Z)),
        (0, 2, 1, -1, (FAR_DOWN, FAR_Z)),
    ]
    conv = conv_weight.reshape(conv_weight.shape[:2] + (-1,))
    up_turned = jnp.transpose(up_weight, (0, 2, 1))

    def layer_of(level, block, known, out_rows):
        up = shift(block, "gy", 1)
        down = shift(block, "gy", -1)
        right, near0, near1, near2 = known
        made = gather_call(
            0,
            level,
            ints,
            flts,
            own,
            frame,
            [block],
            right,
            near0,
            None,
            [up_turned, up_bias, down_bias],
            out_rows,
        )
        acc, made = made[0], list(made[1:])
        if level == 0:
            right, near0 = made[:2]
        ready = made[-3:]
        acc, up, down = lax.optimization_barrier((acc, up, down))
        trio = jnp.stack([block, up, down])
        far = crossing(trio, "gz")
        close = partner(trio, "gz")
        made = gather_call(
            1, level, ints, flts, sides, frame, [up, down, close], right, near1, acc, [], out_rows
        )
        acc = made[0]
        if level == 0:
            near1 = made[1]
        made = gather_call(
            2,
            level,
            ints,
            flts,
            cross,
            frame,
            [far],
            right,
            near2,
            acc,
            [block, conv, down_weight] + ready,
            out_rows,
        )
        if level == 0:
            near2 = made[1]
        return made[0], (right, near0, near1, near2)

    mid, known = layer_of(0, frame, (None,) * 4, mid_rows)
    moved, _ = layer_of(1, mid, known, slot_rows)
    return moved[:, None, None]


def solution(mesh):
    placed = (P("gx", "gy", "gz", None, None),) * 2 + (P("gx", "gy", "gz"),) + (P(),) * 8
    return jax.shard_map(
        local,
        mesh=mesh,
        in_specs=placed,
        out_specs=P("gx", "gy", "gz", None, None),
        check_vma=False,
    )
```

```python
import math

import jax
import jax.numpy as jnp
from jax import lax
from jax.experimental import pallas as pl
from jax.experimental.pallas import tpu as pltpu
from jax.sharding import PartitionSpec as P

EPSILON = 1e-05
FAR = float(2**20)
LOG2E = math.log2(math.e)
HEAD = 8
TERMS = 48
VMEM_LIMIT = 32 * 2**20

MID_START, MID_STOP, LOW, HIGH, MID_AT, OUT_START, OUT_STOP, CUT, COLUMN = range(9)
STEP_Y, STEP_Z, FAR_Y, FAR_Z = 4, 5, 6, 7


def whole():
    return pl.BlockSpec(memory_space=pltpu.VMEM)


def scalars():
    return pl.BlockSpec(memory_space=pltpu.SMEM)


def params():
    return pltpu.CompilerParams(vmem_limit_bytes=VMEM_LIMIT)


def shift(block, axis, by):
    count = lax.axis_size(axis)
    return lax.ppermute(block, axis, [(i, (i + by) % count) for i in range(count)])


def partner(block, axis):
    count = lax.axis_size(axis)
    return lax.ppermute(block, axis, [(i, i ^ 1) for i in range(count)])


def whole_swap(block, other):
    axes = ("gx", "gy", "gz")
    sizes = [lax.axis_size(axis) for axis in axes]
    pairs = []
    for gx in range(sizes[0]):
        for gy in range(sizes[1]):
            for gz in range(sizes[2]):
                px, py, pz = other(gx, gy, gz, sizes)
                here = (gx * sizes[1] + gy) * sizes[2] + gz
                pairs.append((here, (px * sizes[1] + py) * sizes[2] + pz))
    return lax.ppermute(block, axes, pairs)


def beside(index):
    return ((index + 1) ^ 1) - 1


def other_y(gx, gy, gz, sizes):
    if 0 < gy < sizes[1] - 1:
        return gx, beside(gy), gz
    return gx, gy, gz ^ 1


def other_z(gx, gy, gz, sizes):
    if 0 < gz < sizes[2] - 1:
        return gx, gy, beside(gz)
    return gx ^ 1, gy, gz


def split3(value):
    first = value.astype(jnp.bfloat16).astype(jnp.float32)
    rest = value - first
    second = rest.astype(jnp.bfloat16).astype(jnp.float32)
    return first, second, rest - second


def pack(features, positions, counts, old_cuts, new_cuts, rates, rows):
    slot_rows, _, _, width, slots = features.shape
    peers = lax.axis_size("gx")
    last_y = lax.axis_size("gy") - 1
    last_z = lax.axis_size("gz") - 1
    total = peers * slot_rows // 2

    def body(feat_ref, pos_ref, count_ref, old_ref, new_ref, rate_ref, out_ref, int_ref, flt_ref, sem):
        copy = pltpu.make_async_copy(
            feat_ref.at[0:rows, 0, 0], out_ref.at[:, 0:width, :], sem
        )
        copy.start()
        column, row_y, row_z = (lax.axis_index(axis) for axis in ("gx", "gy", "gz"))
        new_low, new_high = new_ref[column], new_ref[column + 1]
        if peers == 2:
            base, mid_at = 0, column
        else:
            base, mid_at = new_low - 2, 1
        int_ref[MID_START] = jnp.maximum(new_low - 1, 0) - base
        int_ref[MID_STOP] = jnp.minimum(new_high + 1, total) - base
        int_ref[LOW] = jnp.int32(0) - base
        int_ref[HIGH] = jnp.int32(total) - base
        int_ref[MID_AT] = jnp.int32(mid_at)
        int_ref[OUT_START] = new_low - base
        int_ref[OUT_STOP] = new_high - base
        int_ref[CUT] = old_ref[1]
        int_ref[COLUMN] = column
        for k in range(2):
            for m in range(2):
                flt_ref[2 * k + m] = rate_ref[k, m]
        flt_ref[STEP_Z] = jnp.where(row_z % 2 == 1, -1.0, 1.0)
        flt_ref[STEP_Y] = jnp.where(row_y % 2 == 1, -1.0, 1.0)
        flt_ref[FAR_Y] = jnp.where(jnp.logical_or(row_y == 0, row_y == last_y), FAR, 0.0)
        flt_ref[FAR_Z] = jnp.where(jnp.logical_or(row_z == 0, row_z == last_z), FAR, 0.0)
        lane = lax.broadcasted_iota(jnp.int32, (1, slots), 1)
        spare = jnp.zeros((HEAD - 4, slots), jnp.float32)
        for row in range(rows):
            place = [pos_ref[d, row : row + 1, :].astype(jnp.float32) for d in range(3)]
            far = jnp.where(lane < count_ref[row], 0.0, FAR)
            block = jnp.concatenate(place + [far, spare], axis=0)
            out_ref[row, width : width + HEAD, :] = block.astype(jnp.bfloat16)
        copy.wait()

    return pl.pallas_call(
        body,
        out_shape=(
            jax.ShapeDtypeStruct((rows, width + HEAD, slots), jnp.bfloat16),
            jax.ShapeDtypeStruct((9,), jnp.int32),
            jax.ShapeDtypeStruct((8,), jnp.float32),
        ),
        in_specs=[pl.BlockSpec(memory_space=pl.ANY), whole()] + [scalars()] * 4,
        out_specs=(whole(), scalars(), scalars()),
        scratch_shapes=[pltpu.SemaphoreType.DMA],
    )(
        features,
        jnp.transpose(positions[:, 0, 0], (1, 0, 2)),
        counts.reshape(-1),
        old_cuts,
        new_cuts,
        rates,
    )


def assemble(ints, mine, other, rows):
    def body(int_ref, mine_ref, other_ref, out_ref):
        cut, column = int_ref[CUT], int_ref[COLUMN]
        for row in range(rows):
            owner = jnp.int32(row) >= cut
            place = jnp.where(owner, row - cut, row)
            place = jnp.clip(place, 0, mine_ref.shape[0] - 1)
            is_mine = owner.astype(jnp.int32) == column
            out_ref[row] = jnp.where(is_mine, mine_ref[place], other_ref[place])

    return pl.pallas_call(
        body,
        out_shape=jax.ShapeDtypeStruct((rows,) + mine.shape[1:], mine.dtype),
        in_specs=[scalars(), whole(), whole()],
        out_specs=whole(),
        compiler_params=params(),
    )(ints, mine, other)


def centre_terms(place, along, row8):
    here = place.astype(jnp.float32)
    live = row8 < 3
    at = jnp.where(row8 == 0, here + along, jnp.where(live, here, 0.0))
    n1, n2, n3 = split3(jnp.sum(at * at, axis=0, keepdims=True))
    minus = jnp.where(live, -2.0 * here, 0.0)
    norm = jnp.where(row8 == 4, n1, jnp.where(row8 == 5, n2, jnp.where(row8 == 6, n3, 0.0)))
    turned = jnp.sum(jnp.where(row8 == 0, minus, 0.0), axis=0, keepdims=True)
    lead = jnp.where(row8 == 3, 1.0, jnp.where(row8 == 7, turned, minus + norm))
    other = jnp.where(jnp.logical_or(row8 == 0, row8 == 3), -2.0 * along, minus)
    ones = jnp.where(live, 1.0, 0.0)
    stack = jnp.concatenate([lead, other, ones, ones, ones, jnp.zeros_like(ones)], axis=0)
    return stack.T.astype(jnp.bfloat16)


def near_terms(place, base, along, gone, row8):
    move = jnp.where(row8 == 3, base - gone, jnp.where(row8 == 7, -along, base))
    there = place.astype(jnp.float32) - move
    first = there.astype(jnp.bfloat16).astype(jnp.float32)
    rest = there - first
    second = jnp.where(row8 == 0, there, jnp.where(row8 == 3, along, rest))
    at = jnp.where(row8 == 0, there + along, jnp.where(row8 < 3, there, 0.0))
    q1, q2, q3 = split3(at * at)
    stack = jnp.concatenate([first, second, q1, q2, q3, jnp.zeros_like(q1)], axis=0)
    return stack.astype(jnp.bfloat16)


def gather_bins(rows, scales, near_ref, feats, right_ref, feat_at):
    sums = []
    for row in rows:
        right = right_ref[row]
        items = [(c, dx) for c in range(len(feats)) for dx in range(3)]
        total = None
        for k in range(0, len(items), 2):
            lefts = []
            vals = []
            for c, dx in items[k : k + 2]:
                lefts.append(near_ref[c, row + dx])
                source = jnp.clip(row + dx - 1 - feat_at, 0, feats[c].shape[0] - 1)
                vals.append(feats[c][source, :, :])
            left = lefts[0] if len(lefts) == 1 else jnp.concatenate(lefts, axis=1)
            feat = vals[0] if len(vals) == 1 else jnp.concatenate(vals, axis=1)
            dist = jnp.dot(right, left, preferred_element_type=jnp.float32)
            weight = jnp.concatenate(
                [jnp.exp2(dist * scale).astype(jnp.bfloat16) for scale in scales], axis=0
            )
            part = lax.dot_general(
                feat, weight, (((1,), (1,)), ((), ())), preferred_element_type=jnp.float32
            )
            total = part if total is None else total + part
        sums.append(total)
    return sums


def views(spec, arrays, start, size):
    found = []
    for index, sub, *_ in spec:
        ref = arrays[index] if sub is None else arrays[index].at[sub]
        found.append(ref.at[:, start : start + size, :])
    return found


def gather_call(stage, level, ints, flts, spec, frame, feats, right, near, before, extra, out_rows):
    frame_rows, tall, slots = frame.shape
    features = tall - HEAD
    centre = frame_rows // 2
    make_right = right is None
    make_near = near is None
    inputs = [frame] + list(feats)
    if not make_right:
        inputs.append(right)
    if not make_near:
        inputs.append(near)
    if before is not None:
        inputs.append(before)
    inputs += list(extra)
    outs = []
    wide = 2 * slots
    if stage < 2:
        outs.append(jax.ShapeDtypeStruct((out_rows, features, wide), jnp.float32))
    else:
        outs.append(jax.ShapeDtypeStruct((out_rows, features, slots), jnp.bfloat16))
    if make_right:
        outs.append(jax.ShapeDtypeStruct((frame_rows, slots, TERMS), jnp.bfloat16))
    if make_near:
        outs.append(
            jax.ShapeDtypeStruct((len(spec), frame_rows + 2, TERMS, slots), jnp.bfloat16)
        )
    if stage == 0:
        hid = extra[0].shape[2]
        outs.append(jax.ShapeDtypeStruct((hid, features), jnp.bfloat16))
        outs.append(jax.ShapeDtypeStruct((hid, wide), jnp.float32))
        outs.append(jax.ShapeDtypeStruct((features, wide), jnp.float32))

    def body(*refs):
        refs = list(refs)
        ints, flts = refs.pop(0), refs.pop(0)
        home = refs.pop(0)
        vals = [refs.pop(0) for _ in feats]
        right_ref = None if make_right else refs.pop(0)
        near_ref = None if make_near else refs.pop(0)
        prior = None if before is None else refs.pop(0)
        extras = [refs.pop(0) for _ in extra]
        out_ref = refs.pop(0)
        right_ref = refs.pop(0) if make_right else right_ref
        near_ref = refs.pop(0) if make_near else near_ref
        start, stop = (
            (ints[MID_START], ints[MID_STOP]) if level == 0 else (ints[OUT_START], ints[OUT_STOP])
        )
        out_at = ints[MID_AT] if level == 0 else ints[OUT_START]
        feat_at = jnp.int32(0) if level == 0 else ints[MID_AT]
        row8 = lax.broadcasted_iota(jnp.int32, (HEAD, slots), 0)
        scales = [flts[2 * level + m] * -LOG2E for m in range(2)]

        if make_right:
            for row in range(frame_rows):
                place = home[row, features:tall, :]
                right_ref[row] = centre_terms(place, float(centre - row), row8)
        if make_near:
            edge = jnp.where(row8 == 3, FAR, 0.0)
            edge = jnp.concatenate([edge] + [jnp.zeros_like(edge)] * (TERMS // HEAD - 1), axis=0)
            edge = edge.astype(jnp.bfloat16)
            wheres = views(spec, vals, features, HEAD)
            for c, (_, _, dy, dz, flags) in enumerate(spec):
                near_ref[c, 0] = edge
                near_ref[c, frame_rows + 1] = edge
                gone = jnp.float32(0.0)
                for flag in flags:
                    gone = gone + flts[flag]
                base = jnp.where(row8 == 1, float(dy) * flts[STEP_Y], 0.0)
                base = jnp.where(row8 == 2, float(dz) * flts[STEP_Z], base)
                base = jnp.where(jnp.logical_and(row8 >= 4, row8 <= 6), -1.0, base)
                for row in range(frame_rows):
                    inside = jnp.logical_and(row >= ints[LOW], row < ints[HIGH])
                    lost = gone + jnp.where(inside, 0.0, FAR)
                    near_ref[c, row + 1] = near_terms(
                        wheres[c][row, :, :], base, float(centre - row), lost, row8
                    )
        heads = views(spec, vals, 0, features)

        if stage == 0:
            up_ref, upb_ref, downb_ref = extras
            wup_ref, wupb_ref, wdownb_ref = refs[:3]
            wup_ref[...] = up_ref[level].astype(jnp.float32).T.astype(jnp.bfloat16)
            lift = jnp.broadcast_to(upb_ref[level : level + 1, :], (slots, upb_ref.shape[1])).T
            wupb_ref[...] = jnp.concatenate([lift, lift], axis=1)
            low = jnp.broadcast_to(downb_ref[level : level + 1, :], (slots, features))
            low = jnp.concatenate([low, low], axis=1).T[0:features, :]
            wdownb_ref[...] = jnp.concatenate([low, low], axis=1)

        def pair(turn):
            first = start + 2 * turn
            return [first, jnp.minimum(first + 1, stop - 1)]

        turns = (stop - start + 1) // 2
        if stage < 2:

            def step(turn, carry):
                rows = pair(turn)
                sums = gather_bins(rows, scales, near_ref, heads, right_ref, feat_at)
                for row, total in zip(rows, sums):
                    if prior is not None:
                        total = total + prior[row - out_at]
                    out_ref[row - out_at] = total
                return carry

            lax.fori_loop(0, turns, step, 0)
            return

        centre_ref, conv_ref, down_ref, wup_ref, wupb_ref, wdownb_ref = extras
        gath_ref = refs[0]

        def finish(rows, slot):
            mixed = jnp.dot(conv_ref[level], gath_ref[slot], preferred_element_type=jnp.float32)
            centred = mixed - jnp.mean(mixed, axis=0, keepdims=True)
            spread = jnp.mean(centred * centred, axis=0, keepdims=True)
            normed = (centred * lax.rsqrt(spread + EPSILON)).astype(jnp.bfloat16)
            hidden = jnp.dot(wup_ref[...], normed, preferred_element_type=jnp.float32)
            half = 0.5 * (hidden + wupb_ref[...])
            hidden = (half + half * jnp.tanh(half)).astype(jnp.bfloat16)
            update = jnp.dot(down_ref[level], hidden, preferred_element_type=jnp.float32)
            update = update + wdownb_ref[...]
            for k, row in enumerate(rows):
                source = jnp.clip(row - feat_at, 0, centre_ref.shape[0] - 1)
                kept = centre_ref[source, 0:features, :].astype(jnp.float32)
                far = home[row, features:tall, :].astype(jnp.float32)[3:4, :]
                result = kept + update[:, k * slots : (k + 1) * slots]
                out_ref[row - out_at] = jnp.where(far == 0.0, result, 0.0).astype(jnp.bfloat16)

        for place in range(out_rows):
            out_ref[place] = jnp.zeros((features, slots), jnp.bfloat16)

        def step(turn, carry):
            rows = pair(turn)
            sums = gather_bins(rows, scales, near_ref, heads, right_ref, feat_at)
            finish(pair(jnp.maximum(turn - 1, 0)), (turn + 1) % 2)
            both = []
            for row, total in zip(rows, sums):
                total = total + prior[row - out_at]
                both.append(jnp.concatenate([total[:, :slots], total[:, slots:]], axis=0))
            gath_ref[turn % 2] = jnp.concatenate(both, axis=1).astype(jnp.bfloat16)
            return carry

        lax.fori_loop(0, turns, step, 0)
        finish(pair(turns - 1), (turns + 1) % 2)

    pairs = out_rows * 3 * len(spec)
    scratch = [pltpu.VMEM((2, 2 * features, wide), jnp.bfloat16)] if stage == 2 else []
    return pl.pallas_call(
        body,
        out_shape=tuple(outs),
        in_specs=[scalars(), scalars()] + [whole()] * len(inputs),
        out_specs=tuple(whole() for _ in outs),
        scratch_shapes=scratch,
        cost_estimate=pl.CostEstimate(
            flops=pairs * 2 * slots * slots * (2 * features + TERMS),
            transcendentals=pairs * 2 * slots * slots,
            bytes_accessed=pairs * 4 * slots * slots,
        ),
        compiler_params=params(),
    )(ints, flts, *inputs)


def local(
    features,
    positions,
    counts,
    old_cuts,
    new_cuts,
    radial_rates,
    conv_weight,
    up_weight,
    up_bias,
    down_weight,
    down_bias,
):
    peers = lax.axis_size("gx")
    slot_rows = features.shape[0]
    total = peers * slot_rows // 2
    most = min(slot_rows, total - 2 * (peers - 1))
    packed, ints, flts = pack(
        features, positions, counts, old_cuts, new_cuts, radial_rates, most
    )

    if peers == 2:
        other = lax.ppermute(packed, "gx", [(0, 1), (1, 0)])
        frame = assemble(ints, packed, other, total)
        mid_rows = total - 1
    else:
        column = lax.axis_index("gx")
        old_low = old_cuts[column]
        old_high = old_cuts[column + 1]
        held = old_high - old_low
        frame_rows = slot_rows + 4
        base = new_cuts[column] - 2
        pieces = [packed]
        starts = [old_low]
        for by, rows in ((1, 3), (2, 1)):
            tail_at = jnp.maximum(held - rows, 0)
            tail = lax.dynamic_slice_in_dim(packed, tail_at, rows, 0)
            pieces.append(shift(tail, "gx", by))
            back = jnp.maximum(column - by, 0)
            starts.append(jnp.maximum(old_cuts[back], old_cuts[back + 1] - rows))
            pieces.append(shift(packed[:rows], "gx", -by))
            starts.append(old_cuts[jnp.minimum(column + by, peers - 1)])
        layer = base + jnp.arange(frame_rows, dtype=jnp.int32)
        before = old_cuts[jnp.maximum(column - 1, 0)]
        after = old_cuts[jnp.minimum(column + 1, peers - 1) + 1]
        at = []
        first = 0
        for piece, begin in zip(pieces, starts):
            at.append(first + layer - begin)
            first += piece.shape[0]
        choice = jnp.where(
            layer >= old_high,
            jnp.where(layer >= after, at[4], at[2]),
            jnp.where(layer >= old_low, at[0], jnp.where(layer >= before, at[1], at[3])),
        )
        frame = jnp.take(jnp.concatenate(pieces, axis=0), jnp.clip(choice, 0, first - 1), axis=0)
        mid_rows = slot_rows + 2

    own = [(0, None, 0, 0, ())]
    sides = [
        (0, None, -1, 0, (FAR_Y,)),
        (1, None, 1, 0, ()),
        (2, 0, 0, 1, ()),
        (2, 1, -1, 1, (FAR_Y,)),
        (2, 2, 1, 1, ()),
    ]
    cross = [
        (0, 0, 0, -1, (FAR_Z,)),
        (0, 1, -1, -1, (FAR_Y, FAR_Z)),
        (0, 2, 1, -1, (FAR_Z,)),
    ]
    conv = conv_weight.reshape(conv_weight.shape[:2] + (-1,))
    up_turned = jnp.transpose(up_weight, (0, 2, 1))

    def layer_of(level, block, known, out_rows):
        up = whole_swap(block, other_y)
        down = partner(block, "gy")
        right, near0, near1, near2 = known
        made = gather_call(
            0,
            level,
            ints,
            flts,
            own,
            frame,
            [block],
            right,
            near0,
            None,
            [up_turned, up_bias, down_bias],
            out_rows,
        )
        acc, made = made[0], list(made[1:])
        if level == 0:
            right, near0 = made[:2]
        ready = made[-3:]
        acc, up, down = lax.optimization_barrier((acc, up, down))
        trio = jnp.stack([block, up, down])
        close = partner(trio, "gz")
        far = whole_swap(trio, other_z)
        made = gather_call(
            1, level, ints, flts, sides, frame, [up, down, close], right, near1, acc, [], out_rows
        )
        acc = made[0]
        if level == 0:
            near1 = made[1]
        made = gather_call(
            2,
            level,
            ints,
            flts,
            cross,
            frame,
            [far],
            right,
            near2,
            acc,
            [block, conv, down_weight] + ready,
            out_rows,
        )
        if level == 0:
            near2 = made[1]
        return made[0], (right, near0, near1, near2)

    mid, known = layer_of(0, frame, (None,) * 4, mid_rows)
    moved, _ = layer_of(1, mid, known, slot_rows)
    return moved[:, None, None]


def solution(mesh):
    placed = (P("gx", "gy", "gz", None, None),) * 2 + (P("gx", "gy", "gz"),) + (P(),) * 8
    return jax.shard_map(
        local,
        mesh=mesh,
        in_specs=placed,
        out_specs=P("gx", "gy", "gz", None, None),
        check_vma=False,
    )
```

```python
import math

import jax
import jax.numpy as jnp
from jax import lax
from jax.experimental import pallas as pl
from jax.experimental.pallas import tpu as pltpu
from jax.sharding import PartitionSpec as P

EPSILON = 1e-05
FAR = float(2**20)
LOG2E = math.log2(math.e)
HEAD = 8
TERMS = 32
VMEM_LIMIT = 32 * 2**20

MID_START, MID_STOP, LOW, HIGH, MID_AT, OUT_START, OUT_STOP, CUT, COLUMN = range(9)
STEP_Y, STEP_Z, FAR_Y, FAR_Z = 4, 5, 6, 7


def whole():
    return pl.BlockSpec(memory_space=pltpu.VMEM)


def scalars():
    return pl.BlockSpec(memory_space=pltpu.SMEM)


def outside(array):
    return pltpu.with_memory_space_constraint(array, pltpu.HBM)


def params():
    return pltpu.CompilerParams(vmem_limit_bytes=VMEM_LIMIT)


def shift(block, axis, by):
    count = lax.axis_size(axis)
    return lax.ppermute(block, axis, [(i, (i + by) % count) for i in range(count)])


def partner(block, axis):
    count = lax.axis_size(axis)
    return lax.ppermute(block, axis, [(i, i ^ 1) for i in range(count)])


def whole_swap(block, other):
    axes = ("gx", "gy", "gz")
    sizes = [lax.axis_size(axis) for axis in axes]
    pairs = []
    for gx in range(sizes[0]):
        for gy in range(sizes[1]):
            for gz in range(sizes[2]):
                px, py, pz = other(gx, gy, gz, sizes)
                here = (gx * sizes[1] + gy) * sizes[2] + gz
                pairs.append((here, (px * sizes[1] + py) * sizes[2] + pz))
    return lax.ppermute(block, axes, pairs)


def beside(index):
    return ((index + 1) ^ 1) - 1


def other_y(gx, gy, gz, sizes):
    if 0 < gy < sizes[1] - 1:
        return gx, beside(gy), gz
    return gx, gy, gz ^ 1


def other_z(gx, gy, gz, sizes):
    if 0 < gz < sizes[2] - 1:
        return gx, gy, beside(gz)
    return gx ^ 1, gy, gz


def split3(value):
    first = value.astype(jnp.bfloat16).astype(jnp.float32)
    rest = value - first
    second = rest.astype(jnp.bfloat16).astype(jnp.float32)
    return first, second, rest - second


def pack(features, positions, counts, old_cuts, new_cuts, rates, rows):
    slot_rows, _, _, width, slots = features.shape
    peers = lax.axis_size("gx")
    last_y = lax.axis_size("gy") - 1
    last_z = lax.axis_size("gz") - 1
    total = peers * slot_rows // 2

    def body(
        feat_ref,
        pos_in,
        count_in,
        old_in,
        new_in,
        rate_in,
        out_ref,
        int_ref,
        flt_ref,
        pos_ref,
        count_ref,
        old_ref,
        new_ref,
        rate_ref,
        sems,
    ):
        copies = [
            pltpu.make_async_copy(source, target, sems.at[k])
            for k, (source, target) in enumerate(
                (
                    (old_in, old_ref),
                    (new_in, new_ref),
                    (rate_in, rate_ref),
                    (count_in, count_ref),
                    (pos_in, pos_ref),
                    (feat_ref.at[0:rows, 0, 0], out_ref.at[:, 0:width, :]),
                )
            )
        ]
        for copy in copies:
            copy.start()
        for copy in copies[:5]:
            copy.wait()
        column, row_y, row_z = (lax.axis_index(axis) for axis in ("gx", "gy", "gz"))
        new_low, new_high = new_ref[column], new_ref[column + 1]
        if peers == 2:
            base, mid_at = 0, column
        else:
            base, mid_at = new_low - 2, 1
        ints = {
            MID_START: jnp.maximum(new_low - 1, 0) - base,
            MID_STOP: jnp.minimum(new_high + 1, total) - base,
            LOW: jnp.int32(0) - base,
            HIGH: jnp.int32(total) - base,
            MID_AT: jnp.int32(mid_at),
            OUT_START: new_low - base,
            OUT_STOP: new_high - base,
            CUT: old_ref[1],
            COLUMN: column,
        }
        flts = {
            STEP_Y: jnp.where(row_y % 2 == 1, -1.0, 1.0),
            STEP_Z: jnp.where(row_z % 2 == 1, -1.0, 1.0),
            FAR_Y: jnp.where(jnp.logical_or(row_y == 0, row_y == last_y), FAR, 0.0),
            FAR_Z: jnp.where(jnp.logical_or(row_z == 0, row_z == last_z), FAR, 0.0),
        }
        for k in range(2):
            for m in range(2):
                flts[2 * k + m] = rate_ref[k, m]
        lane = lax.broadcasted_iota(jnp.int32, (1, slots), 1)
        line = jnp.zeros((1, slots), jnp.int32)
        for k, value in ints.items():
            line = jnp.where(lane == k, value, line)
        int_ref[...] = line
        line = jnp.zeros((1, slots), jnp.float32)
        for k, value in flts.items():
            line = jnp.where(lane == k, value, line)
        below = jnp.ones((1, slots), jnp.float32)
        for k in range(2):
            below = jnp.where(lane == 2 * k + 1, rate_ref[k, 0], below)
        share = line / below
        flt_ref[...] = share + (line - share * below) / below
        spare = jnp.zeros((HEAD - 4, slots), jnp.float32)
        for row in range(rows):
            place = [pos_ref[d, row : row + 1, :].astype(jnp.float32) for d in range(3)]
            far = jnp.where(lane < count_ref[row], 0.0, FAR)
            block = jnp.concatenate(place + [far, spare], axis=0).astype(jnp.bfloat16)
            out_ref[row, width : width + HEAD, :] = block
        copies[5].wait()

    anywhere = pl.BlockSpec(memory_space=pltpu.HBM)
    return pl.pallas_call(
        body,
        out_shape=(
            jax.ShapeDtypeStruct((rows, width + HEAD, slots), jnp.bfloat16),
            jax.ShapeDtypeStruct((1, slots), jnp.int32),
            jax.ShapeDtypeStruct((1, slots), jnp.float32),
        ),
        in_specs=[anywhere] * 6,
        out_specs=(whole(), whole(), whole()),
        scratch_shapes=[
            pltpu.VMEM((3, slot_rows, slots), positions.dtype),
            pltpu.SMEM((slot_rows,), counts.dtype),
            pltpu.SMEM(old_cuts.shape, old_cuts.dtype),
            pltpu.SMEM(new_cuts.shape, new_cuts.dtype),
            pltpu.SMEM(rates.shape, rates.dtype),
            pltpu.SemaphoreType.DMA((6,)),
        ],
        compiler_params=params(),
    )(
        outside(features),
        outside(jnp.transpose(positions[:, 0, 0], (1, 0, 2))),
        outside(counts.reshape(-1)),
        outside(old_cuts),
        outside(new_cuts),
        outside(rates),
    )


def assemble(ints, mine, other, rows):
    def body(int_ref, mine_ref, other_ref, out_ref):
        cut, column = int_ref[0, CUT], int_ref[0, COLUMN]
        for row in range(rows):
            owner = jnp.int32(row) >= cut
            place = jnp.where(owner, row - cut, row)
            place = jnp.clip(place, 0, mine_ref.shape[0] - 1)
            is_mine = owner.astype(jnp.int32) == column
            out_ref[row] = jnp.where(is_mine, mine_ref[place], other_ref[place])

    return pl.pallas_call(
        body,
        out_shape=jax.ShapeDtypeStruct((rows,) + mine.shape[1:], mine.dtype),
        in_specs=[scalars(), whole(), whole()],
        out_specs=whole(),
        compiler_params=params(),
    )(ints, mine, other)


def stacked(blocks):
    def body(*refs):
        for k in range(len(blocks)):
            for row in range(blocks[0].shape[0]):
                refs[-1][k, row] = refs[k][row]

    return pl.pallas_call(
        body,
        out_shape=jax.ShapeDtypeStruct((len(blocks),) + blocks[0].shape, blocks[0].dtype),
        in_specs=[whole()] * len(blocks),
        out_specs=whole(),
        compiler_params=params(),
    )(*blocks)


def centre_terms(place, along, row8, spread):
    here = place.astype(jnp.float32)
    live = row8 < 3
    at = jnp.where(row8 == 0, here + along, jnp.where(live, here, 0.0))
    norm = jnp.sum(at * at, axis=0, keepdims=True)
    rows = jnp.where(row8 == 3, norm, -2.0 * at)
    stack = jnp.concatenate(split3(rows) + (jnp.zeros_like(rows),), axis=0)
    return jnp.dot(stack.T.astype(jnp.bfloat16), spread, preferred_element_type=jnp.float32)


def near_terms(place, base, along, gone, row8):
    there = place.astype(jnp.float32)
    far = there[3:4, :] + gone
    at = jnp.where(row8 == 0, there + along, jnp.where(row8 < 3, there - base, 0.0))
    norm = jnp.sum(at * at, axis=0, keepdims=True)
    norm = jnp.where(far > 0.0, FAR * FAR, norm)
    return jnp.where(row8 == 3, norm, at)


def gather_bins(rows, scales, near_ref, feats, centre_ref, feat_at):
    sums = []
    scale, ratio = scales
    for row in rows:
        minus = [centre_ref[row, k] for k in range(3)]
        norm = centre_ref[row, 3] * scale
        items = [(c, dx) for c in range(len(feats)) for dx in range(3)]
        total = None
        for k in range(0, len(items), 2):
            weights = [[], []]
            vals = []
            for c, dx in items[k : k + 2]:
                near = near_ref[c, row + dx] * scale
                power = norm + near[3:4, :]
                for d in range(3):
                    power = power + minus[d] * near[d : d + 1, :]
                weights[0].append(jnp.exp2(power).astype(jnp.bfloat16))
                weights[1].append(jnp.exp2(power * ratio).astype(jnp.bfloat16))
                source = jnp.clip(row + dx - 1 - feat_at, 0, feats[c].shape[0] - 1)
                vals.append(feats[c][source, :, :])
            if len(vals) == 1:
                feat = vals[0]
                sides = [group[0] for group in weights]
            else:
                feat = jnp.concatenate(vals, axis=1)
                sides = [jnp.concatenate(group, axis=1) for group in weights]
            part = lax.dot_general(
                feat,
                jnp.concatenate(sides, axis=0),
                (((1,), (1,)), ((), ())),
                preferred_element_type=jnp.float32,
            )
            total = part if total is None else total + part
        sums.append(total)
    return sums


def views(spec, arrays, start, size):
    found = []
    for index, sub, *_ in spec:
        ref = arrays[index] if sub is None else arrays[index].at[sub]
        found.append(ref.at[:, start : start + size, :])
    return found


def gather_call(stage, level, ints, flts, spec, frame, feats, right, near, before, extra, out_rows):
    frame_rows, tall, slots = frame.shape
    features = tall - HEAD
    centre = frame_rows // 2
    make_right = right is None
    make_near = near is None
    inputs = [frame] + list(feats)
    if not make_right:
        inputs.append(right)
    if not make_near:
        inputs.append(near)
    if before is not None:
        inputs.append(before)
    inputs += list(extra)
    outs = []
    wide = 2 * slots
    if stage < 2:
        outs.append(jax.ShapeDtypeStruct((out_rows, features, wide), jnp.float32))
    else:
        outs.append(jax.ShapeDtypeStruct((out_rows, features, slots), jnp.bfloat16))
    if make_right:
        outs.append(jax.ShapeDtypeStruct((frame_rows, 4, slots, slots), jnp.float32))
    if make_near:
        outs.append(
            jax.ShapeDtypeStruct((len(spec), frame_rows + 2, HEAD, slots), jnp.float32)
        )
    if stage == 0:
        hid = extra[0].shape[2]
        outs.append(jax.ShapeDtypeStruct((features, 2 * features), jnp.bfloat16))
        outs.append(jax.ShapeDtypeStruct((hid, features), jnp.bfloat16))
        outs.append(jax.ShapeDtypeStruct((hid, wide), jnp.float32))
        outs.append(jax.ShapeDtypeStruct((features, wide), jnp.float32))

    def body(*refs):
        refs = list(refs)
        ints, flts = refs.pop(0).at[0], refs.pop(0).at[0]
        home = refs.pop(0)
        vals = [refs.pop(0) for _ in feats]
        right_ref = None if make_right else refs.pop(0)
        near_ref = None if make_near else refs.pop(0)
        prior = None if before is None else refs.pop(0)
        extras = [refs.pop(0) for _ in extra]
        out_ref = refs.pop(0)
        right_ref = refs.pop(0) if make_right else right_ref
        near_ref = refs.pop(0) if make_near else near_ref
        start, stop = (
            (ints[MID_START], ints[MID_STOP]) if level == 0 else (ints[OUT_START], ints[OUT_STOP])
        )
        out_at = ints[MID_AT] if level == 0 else ints[OUT_START]
        feat_at = jnp.int32(0) if level == 0 else ints[MID_AT]
        if stage == 0:
            held = refs[4:8]
            copies = [
                pltpu.make_async_copy(source, target, refs[8].at[k])
                for k, (source, target) in enumerate(zip(extras, held))
            ]
            for copy in copies:
                copy.start()
        row8 = lax.broadcasted_iota(jnp.int32, (HEAD, slots), 0)
        scales = [flts[2 * level] * -LOG2E, flts[2 * level + 1]]

        if make_right:
            kind = lax.broadcasted_iota(jnp.int32, (TERMS, 4 * slots), 0)
            lane = lax.broadcasted_iota(jnp.int32, (TERMS, 4 * slots), 1)
            spread = jnp.where(
                jnp.logical_and(kind % HEAD == lane // slots, kind < 3 * HEAD), 1.0, 0.0
            ).astype(jnp.bfloat16)
            for row in range(frame_rows):
                place = home[row, features:tall, :]
                terms = centre_terms(place, float(centre - row), row8, spread)
                for k in range(4):
                    right_ref[row, k] = terms[:, k * slots : (k + 1) * slots]
        if make_near:
            edge = jnp.where(row8 == 3, FAR * FAR, 0.0)
            wheres = views(spec, vals, features, HEAD)
            for c, (_, _, dy, dz, flags) in enumerate(spec):
                near_ref[c, 0] = edge
                near_ref[c, frame_rows + 1] = edge
                gone = jnp.float32(0.0)
                for flag in flags:
                    gone = gone + flts[flag]
                base = jnp.where(row8 == 1, float(dy) * flts[STEP_Y], 0.0)
                base = jnp.where(row8 == 2, float(dz) * flts[STEP_Z], base)
                for row in range(frame_rows):
                    inside = jnp.logical_and(row >= ints[LOW], row < ints[HIGH])
                    lost = gone + jnp.where(inside, 0.0, FAR)
                    near_ref[c, row + 1] = near_terms(
                        wheres[c][row, :, :], base, float(centre - row), lost, row8
                    )
        heads = views(spec, vals, 0, features)

        def pair(turn):
            return [start + 2 * turn, start + 2 * turn + 1]

        turns = (stop - start) // 2
        odd = (stop - start) % 2
        if stage < 2:

            def gather(rows):
                sums = gather_bins(rows, scales, near_ref, heads, right_ref, feat_at)
                for row, total in zip(rows, sums):
                    if prior is not None:
                        total = total + prior[row - out_at]
                    out_ref[row - out_at] = total

            def step(turn, carry):
                gather(pair(turn))
                return carry

            lax.fori_loop(0, turns, step, 0)

            @pl.when(odd == 1)
            def _():
                gather([stop - 1])

            if stage == 0:
                wconv_ref, wup_ref, wupb_ref, wdownb_ref = refs[:4]
                up_ref, upb_ref, downb_ref, conv_in = held
                for copy in copies:
                    copy.wait()
                wconv_ref[...] = jnp.concatenate(
                    [conv_in[level, :, m, :] for m in range(2)], axis=1
                )
                wup_ref[...] = up_ref[level].astype(jnp.float32).T.astype(jnp.bfloat16)
                lift = jnp.broadcast_to(upb_ref[level : level + 1, :], (slots, upb_ref.shape[1])).T
                wupb_ref[...] = jnp.concatenate([lift, lift], axis=1)
                low = jnp.broadcast_to(downb_ref[level : level + 1, :], (slots, features))
                low = jnp.concatenate([low, low], axis=1).T[0:features, :]
                wdownb_ref[...] = jnp.concatenate([low, low], axis=1)

            return

        centre_ref, down_ref, conv_ref, wup_ref, wupb_ref, wdownb_ref = extras
        gath_ref = refs[0]

        def finish(rows, slot):
            size = len(rows) * slots
            packed = gath_ref[slot, :, 0:size]
            mixed = jnp.dot(conv_ref[...], packed, preferred_element_type=jnp.float32)
            centred = mixed - jnp.mean(mixed, axis=0, keepdims=True)
            spread = jnp.mean(centred * centred, axis=0, keepdims=True)
            normed = (centred * lax.rsqrt(spread + EPSILON)).astype(jnp.bfloat16)
            hidden = jnp.dot(wup_ref[...], normed, preferred_element_type=jnp.float32)
            half = 0.5 * (hidden + wupb_ref[:, 0:size])
            hidden = (half + half * jnp.tanh(half)).astype(jnp.bfloat16)
            update = jnp.dot(down_ref[level], hidden, preferred_element_type=jnp.float32)
            update = update + wdownb_ref[:, 0:size]
            for k, row in enumerate(rows):
                source = jnp.clip(row - feat_at, 0, centre_ref.shape[0] - 1)
                kept = centre_ref[source, 0:features, :].astype(jnp.float32)
                far = home[row, features:tall, :].astype(jnp.float32)[3:4, :]
                result = kept + update[:, k * slots : (k + 1) * slots]
                out_ref[row - out_at] = jnp.where(far == 0.0, result, 0.0).astype(jnp.bfloat16)

        for place in range(out_rows):
            out_ref[place] = jnp.zeros((features, slots), jnp.bfloat16)

        def gather(rows, slot, last):
            sums = gather_bins(rows, scales, near_ref, heads, right_ref, feat_at)
            finish(pair(last), 1 - slot)
            both = []
            for row, total in zip(rows, sums):
                total = total + prior[row - out_at]
                both.append(jnp.concatenate([total[:, :slots], total[:, slots:]], axis=0))
            both = both[0] if len(both) == 1 else jnp.concatenate(both, axis=1)
            gath_ref[slot, :, 0 : len(rows) * slots] = both.astype(jnp.bfloat16)

        def step(turn, carry):
            gather(pair(turn), turn % 2, jnp.maximum(turn - 1, 0))
            return carry

        lax.fori_loop(0, turns, step, 0)

        @pl.when(odd == 1)
        def _():
            gather([stop - 1], turns % 2, turns - 1)
            finish([stop - 1], turns % 2)

        @pl.when(odd == 0)
        def _():
            finish(pair(turns - 1), (turns + 1) % 2)

    pairs = out_rows * 3 * len(spec)
    specs = [whole()] * len(inputs)
    scratch = []
    if stage == 0:
        scratch = [pltpu.VMEM(array.shape, array.dtype) for array in extra]
        scratch.append(pltpu.SemaphoreType.DMA((len(extra),)))
        specs[len(inputs) - len(extra) :] = [pl.BlockSpec(memory_space=pltpu.HBM)] * len(extra)
    if stage == 2:
        scratch = [pltpu.VMEM((2, 2 * features, wide), jnp.bfloat16)]
    return pl.pallas_call(
        body,
        out_shape=tuple(outs),
        in_specs=[scalars(), scalars()] + specs,
        out_specs=tuple(whole() for _ in outs),
        scratch_shapes=scratch,
        cost_estimate=pl.CostEstimate(
            flops=pairs * 2 * slots * slots * (2 * features + HEAD),
            transcendentals=pairs * 2 * slots * slots,
            bytes_accessed=pairs * 4 * slots * slots,
        ),
        compiler_params=params(),
    )(ints, flts, *inputs)


def local(
    features,
    positions,
    counts,
    old_cuts,
    new_cuts,
    radial_rates,
    conv_weight,
    up_weight,
    up_bias,
    down_weight,
    down_bias,
):
    peers = lax.axis_size("gx")
    slot_rows = features.shape[0]
    total = peers * slot_rows // 2
    most = min(slot_rows, total - 2 * (peers - 1))
    packed, ints, flts = pack(
        features, positions, counts, old_cuts, new_cuts, radial_rates, most
    )

    if peers == 2:
        other = lax.ppermute(packed, "gx", [(0, 1), (1, 0)])
        frame = assemble(ints, packed, other, total)
        mid_rows = total - 1
    else:
        column = lax.axis_index("gx")
        old_low = old_cuts[column]
        old_high = old_cuts[column + 1]
        held = old_high - old_low
        frame_rows = slot_rows + 4
        base = new_cuts[column] - 2
        pieces = [packed]
        starts = [old_low]
        for by, rows in ((1, 3), (2, 1)):
            tail_at = jnp.maximum(held - rows, 0)
            tail = lax.dynamic_slice_in_dim(packed, tail_at, rows, 0)
            pieces.append(shift(tail, "gx", by))
            back = jnp.maximum(column - by, 0)
            starts.append(jnp.maximum(old_cuts[back], old_cuts[back + 1] - rows))
            pieces.append(shift(packed[:rows], "gx", -by))
            starts.append(old_cuts[jnp.minimum(column + by, peers - 1)])
        layer = base + jnp.arange(frame_rows, dtype=jnp.int32)
        before = old_cuts[jnp.maximum(column - 1, 0)]
        after = old_cuts[jnp.minimum(column + 1, peers - 1) + 1]
        at = []
        first = 0
        for piece, begin in zip(pieces, starts):
            at.append(first + layer - begin)
            first += piece.shape[0]
        choice = jnp.where(
            layer >= old_high,
            jnp.where(layer >= after, at[4], at[2]),
            jnp.where(layer >= old_low, at[0], jnp.where(layer >= before, at[1], at[3])),
        )
        frame = jnp.take(jnp.concatenate(pieces, axis=0), jnp.clip(choice, 0, first - 1), axis=0)
        mid_rows = slot_rows + 2

    own = [(0, None, 0, 0, ())]
    sides = [
        (0, None, -1, 0, (FAR_Y,)),
        (1, None, 1, 0, ()),
        (2, 0, 0, 1, ()),
        (2, 1, -1, 1, (FAR_Y,)),
        (2, 2, 1, 1, ()),
    ]
    cross = [
        (0, 0, 0, -1, (FAR_Z,)),
        (0, 1, -1, -1, (FAR_Y, FAR_Z)),
        (0, 2, 1, -1, (FAR_Z,)),
    ]
    up_turned = jnp.transpose(up_weight, (0, 2, 1))

    def layer_of(level, block, known, out_rows):
        up = whole_swap(block, other_y)
        down = partner(block, "gy")
        right, near0, near1, near2 = known
        made = gather_call(
            0,
            level,
            ints,
            flts,
            own,
            frame,
            [block],
            right,
            near0,
            None,
            [outside(array) for array in (up_turned, up_bias, down_bias, conv_weight)],
            out_rows,
        )
        acc, made = made[0], list(made[1:])
        if level == 0:
            right, near0 = made[:2]
        ready = made[-4:]
        acc, up, down = lax.optimization_barrier((acc, up, down))
        trio = stacked([block, up, down])
        close = partner(trio, "gz")
        far = whole_swap(trio, other_z)
        made = gather_call(
            1, level, ints, flts, sides, frame, [up, down, close], right, near1, acc, [], out_rows
        )
        acc = made[0]
        if level == 0:
            near1 = made[1]
        made = gather_call(
            2,
            level,
            ints,
            flts,
            cross,
            frame,
            [far],
            right,
            near2,
            acc,
            [block, down_weight] + ready,
            out_rows,
        )
        if level == 0:
            near2 = made[1]
        return made[0], (right, near0, near1, near2)

    mid, known = layer_of(0, frame, (None,) * 4, mid_rows)
    moved, _ = layer_of(1, mid, known, slot_rows)
    return moved[:, None, None]


def solution(mesh):
    placed = (P("gx", "gy", "gz", None, None),) * 2 + (P("gx", "gy", "gz"),) + (P(),) * 8
    return jax.shard_map(
        local,
        mesh=mesh,
        in_specs=placed,
        out_specs=P("gx", "gy", "gz", None, None),
        check_vma=False,
    )
```

```python
import math

import jax
import jax.numpy as jnp
from jax import lax
from jax.experimental import pallas as pl
from jax.experimental.pallas import tpu as pltpu
from jax.sharding import PartitionSpec as P

EPSILON = 1e-05
FAR = float(2**20)
LOG2E = math.log2(math.e)
HEAD = 8
TERMS = 32
VMEM_LIMIT = 32 * 2**20

MID_START, MID_STOP, LOW, HIGH, MID_AT, OUT_START, OUT_STOP, CUT, COLUMN = range(9)
STEP_Y, STEP_Z, FAR_Y, FAR_Z = 4, 5, 6, 7


def whole():
    return pl.BlockSpec(memory_space=pltpu.VMEM)


def scalars():
    return pl.BlockSpec(memory_space=pltpu.SMEM)


def outside(array):
    return pltpu.with_memory_space_constraint(array, pltpu.HBM)


def params():
    return pltpu.CompilerParams(vmem_limit_bytes=VMEM_LIMIT)


def shift(block, axis, by):
    count = lax.axis_size(axis)
    return lax.ppermute(block, axis, [(i, (i + by) % count) for i in range(count)])


def partner(block, axis):
    count = lax.axis_size(axis)
    return lax.ppermute(block, axis, [(i, i ^ 1) for i in range(count)])


def whole_swap(block, other):
    axes = ("gx", "gy", "gz")
    sizes = [lax.axis_size(axis) for axis in axes]
    pairs = []
    for gx in range(sizes[0]):
        for gy in range(sizes[1]):
            for gz in range(sizes[2]):
                px, py, pz = other(gx, gy, gz, sizes)
                here = (gx * sizes[1] + gy) * sizes[2] + gz
                pairs.append((here, (px * sizes[1] + py) * sizes[2] + pz))
    return lax.ppermute(block, axes, pairs)


def beside(index):
    return ((index + 1) ^ 1) - 1


def other_y(gx, gy, gz, sizes):
    if 0 < gy < sizes[1] - 1:
        return gx, beside(gy), gz
    return gx, gy, gz ^ 1


def other_z(gx, gy, gz, sizes):
    if 0 < gz < sizes[2] - 1:
        return gx, gy, beside(gz)
    return gx ^ 1, gy, gz


def split3(value):
    first = value.astype(jnp.bfloat16).astype(jnp.float32)
    rest = value - first
    second = rest.astype(jnp.bfloat16).astype(jnp.float32)
    return first, second, rest - second


def pack(features, positions, counts, old_cuts, new_cuts, rates, rows):
    slot_rows, _, _, width, slots = features.shape
    peers = lax.axis_size("gx")
    last_y = lax.axis_size("gy") - 1
    last_z = lax.axis_size("gz") - 1
    total = peers * slot_rows // 2

    def body(
        feat_ref,
        pos_in,
        count_in,
        old_in,
        new_in,
        rate_in,
        out_ref,
        int_ref,
        flt_ref,
        pos_ref,
        count_ref,
        old_ref,
        new_ref,
        rate_ref,
        sems,
    ):
        copies = [
            pltpu.make_async_copy(source, target, sems.at[k])
            for k, (source, target) in enumerate(
                (
                    (old_in, old_ref),
                    (new_in, new_ref),
                    (rate_in, rate_ref),
                    (count_in, count_ref),
                    (pos_in, pos_ref),
                    (feat_ref.at[0:rows, 0, 0], out_ref.at[:, 0:width, :]),
                )
            )
        ]
        for copy in copies:
            copy.start()
        for copy in copies[:5]:
            copy.wait()
        column, row_y, row_z = (lax.axis_index(axis) for axis in ("gx", "gy", "gz"))
        new_low, new_high = new_ref[column], new_ref[column + 1]
        if peers == 2:
            base, mid_at = 0, column
        else:
            base, mid_at = new_low - 2, 1
        ints = {
            MID_START: jnp.maximum(new_low - 1, 0) - base,
            MID_STOP: jnp.minimum(new_high + 1, total) - base,
            LOW: jnp.int32(0) - base,
            HIGH: jnp.int32(total) - base,
            MID_AT: jnp.int32(mid_at),
            OUT_START: new_low - base,
            OUT_STOP: new_high - base,
            CUT: old_ref[1],
            COLUMN: column,
        }
        flts = {
            STEP_Y: jnp.where(row_y % 2 == 1, -1.0, 1.0),
            STEP_Z: jnp.where(row_z % 2 == 1, -1.0, 1.0),
            FAR_Y: jnp.where(jnp.logical_or(row_y == 0, row_y == last_y), FAR, 0.0),
            FAR_Z: jnp.where(jnp.logical_or(row_z == 0, row_z == last_z), FAR, 0.0),
        }
        for k in range(2):
            for m in range(2):
                flts[2 * k + m] = rate_ref[k, m]
        lane = lax.broadcasted_iota(jnp.int32, (1, slots), 1)
        line = jnp.zeros((1, slots), jnp.int32)
        for k, value in ints.items():
            line = jnp.where(lane == k, value, line)
        int_ref[...] = line
        line = jnp.zeros((1, slots), jnp.float32)
        for k, value in flts.items():
            line = jnp.where(lane == k, value, line)
        below = jnp.ones((1, slots), jnp.float32)
        for k in range(2):
            below = jnp.where(lane == 2 * k + 1, rate_ref[k, 0], below)
        share = line / below
        flt_ref[...] = share + (line - share * below) / below
        spare = jnp.zeros((HEAD - 4, slots), jnp.float32)
        for row in range(rows):
            place = [pos_ref[d, row : row + 1, :].astype(jnp.float32) for d in range(3)]
            far = jnp.where(lane < count_ref[row], 0.0, FAR)
            block = jnp.concatenate(place + [far, spare], axis=0).astype(jnp.bfloat16)
            out_ref[row, width : width + HEAD, :] = block
        copies[5].wait()

    anywhere = pl.BlockSpec(memory_space=pltpu.HBM)
    return pl.pallas_call(
        body,
        out_shape=(
            jax.ShapeDtypeStruct((rows, width + HEAD, slots), jnp.bfloat16),
            jax.ShapeDtypeStruct((1, slots), jnp.int32),
            jax.ShapeDtypeStruct((1, slots), jnp.float32),
        ),
        in_specs=[anywhere] * 6,
        out_specs=(whole(), whole(), whole()),
        scratch_shapes=[
            pltpu.VMEM((3, slot_rows, slots), positions.dtype),
            pltpu.SMEM((slot_rows,), counts.dtype),
            pltpu.SMEM(old_cuts.shape, old_cuts.dtype),
            pltpu.SMEM(new_cuts.shape, new_cuts.dtype),
            pltpu.SMEM(rates.shape, rates.dtype),
            pltpu.SemaphoreType.DMA((6,)),
        ],
        compiler_params=params(),
    )(
        outside(features),
        outside(jnp.transpose(positions[:, 0, 0], (1, 0, 2))),
        outside(counts.reshape(-1)),
        outside(old_cuts),
        outside(new_cuts),
        outside(rates),
    )


def assemble(ints, mine, other, rows):
    def body(int_ref, mine_ref, other_ref, out_ref):
        cut, column = int_ref[0, CUT], int_ref[0, COLUMN]
        for row in range(rows):
            owner = jnp.int32(row) >= cut
            place = jnp.where(owner, row - cut, row)
            place = jnp.clip(place, 0, mine_ref.shape[0] - 1)
            is_mine = owner.astype(jnp.int32) == column
            out_ref[row] = jnp.where(is_mine, mine_ref[place], other_ref[place])

    return pl.pallas_call(
        body,
        out_shape=jax.ShapeDtypeStruct((rows,) + mine.shape[1:], mine.dtype),
        in_specs=[scalars(), whole(), whole()],
        out_specs=whole(),
        compiler_params=params(),
    )(ints, mine, other)


def stacked(block, up, down):
    def body(block_ref, up_ref, down_ref, trio_ref, rims_ref):
        for row in range(block.shape[0]):
            trio_ref[0, row] = block_ref[row]
            for k, ref in enumerate((up_ref, down_ref)):
                value = ref[row]
                trio_ref[k + 1, row] = value
                rims_ref[k, row] = value

    return pl.pallas_call(
        body,
        out_shape=tuple(
            jax.ShapeDtypeStruct((count,) + block.shape, block.dtype) for count in (3, 2)
        ),
        in_specs=[whole()] * 3,
        out_specs=(whole(), whole()),
        compiler_params=params(),
    )(block, up, down)


def centre_terms(place, along, row8, spread):
    here = place.astype(jnp.float32)
    live = row8 < 3
    at = jnp.where(row8 == 0, here + along, jnp.where(live, here, 0.0))
    norm = jnp.sum(at * at, axis=0, keepdims=True)
    rows = jnp.where(row8 == 3, norm, -2.0 * at)
    stack = jnp.concatenate(split3(rows) + (jnp.zeros_like(rows),), axis=0)
    return jnp.dot(stack.T.astype(jnp.bfloat16), spread, preferred_element_type=jnp.float32)


def near_terms(place, base, along, gone, row8):
    there = place.astype(jnp.float32)
    far = there[3:4, :] + gone
    at = jnp.where(row8 == 0, there + along, jnp.where(row8 < 3, there - base, 0.0))
    norm = jnp.sum(at * at, axis=0, keepdims=True)
    norm = jnp.where(far > 0.0, FAR * FAR, norm)
    return jnp.where(row8 == 3, norm, at)


def gather_bins(rows, scales, near_ref, feats, centre_ref, feat_at):
    sums = []
    scale, ratio = scales
    for row in rows:
        minus = [centre_ref[row, k] for k in range(3)]
        norm = centre_ref[row, 3] * scale
        items = [(c, dx) for c in range(len(feats)) for dx in range(3)]
        total = None
        for k in range(0, len(items), 2):
            weights = [[], []]
            vals = []
            for c, dx in items[k : k + 2]:
                near = near_ref[c, row + dx] * scale
                power = norm + near[3:4, :]
                for d in range(3):
                    power = power + minus[d] * near[d : d + 1, :]
                weights[0].append(jnp.exp2(power).astype(jnp.bfloat16))
                weights[1].append(jnp.exp2(power * ratio).astype(jnp.bfloat16))
                source = jnp.clip(row + dx - 1 - feat_at, 0, feats[c].shape[0] - 1)
                vals.append(feats[c][source, :, :])
            if len(vals) == 1:
                feat = vals[0]
                sides = [group[0] for group in weights]
            else:
                feat = jnp.concatenate(vals, axis=1)
                sides = [jnp.concatenate(group, axis=1) for group in weights]
            part = lax.dot_general(
                feat,
                jnp.concatenate(sides, axis=0),
                (((1,), (1,)), ((), ())),
                preferred_element_type=jnp.float32,
            )
            total = part if total is None else total + part
        sums.append(total)
    return sums


def views(spec, arrays, start, size):
    found = []
    for index, sub, *_ in spec:
        ref = arrays[index] if sub is None else arrays[index].at[sub]
        found.append(ref.at[:, start : start + size, :])
    return found


def gather_call(stage, level, ints, flts, spec, frame, feats, right, near, before, extra, out_rows):
    frame_rows, tall, slots = frame.shape
    features = tall - HEAD
    centre = frame_rows // 2
    make_right = right is None
    make_near = near is None
    inputs = [frame] + list(feats)
    if not make_right:
        inputs.append(right)
    if not make_near:
        inputs.append(near)
    if before is not None:
        inputs.append(before)
    inputs += list(extra)
    outs = []
    wide = 2 * slots
    if stage < 2:
        outs.append(jax.ShapeDtypeStruct((out_rows, features, wide), jnp.float32))
    else:
        outs.append(jax.ShapeDtypeStruct((out_rows, features, slots), jnp.bfloat16))
    if make_right:
        outs.append(jax.ShapeDtypeStruct((frame_rows, 4, slots, slots), jnp.float32))
    if make_near:
        outs.append(
            jax.ShapeDtypeStruct((len(spec), frame_rows + 2, HEAD, slots), jnp.float32)
        )
    if stage == 0:
        hid = extra[0].shape[2]
        outs.append(jax.ShapeDtypeStruct((features, 2 * features), jnp.bfloat16))
        outs.append(jax.ShapeDtypeStruct((hid, features), jnp.bfloat16))
        outs.append(jax.ShapeDtypeStruct((hid, wide), jnp.float32))
        outs.append(jax.ShapeDtypeStruct((features, wide), jnp.float32))

    def body(*refs):
        refs = list(refs)
        ints, flts = refs.pop(0).at[0], refs.pop(0).at[0]
        home = refs.pop(0)
        vals = [refs.pop(0) for _ in feats]
        right_ref = None if make_right else refs.pop(0)
        near_ref = None if make_near else refs.pop(0)
        prior = None if before is None else refs.pop(0)
        extras = [refs.pop(0) for _ in extra]
        out_ref = refs.pop(0)
        right_ref = refs.pop(0) if make_right else right_ref
        near_ref = refs.pop(0) if make_near else near_ref
        start, stop = (
            (ints[MID_START], ints[MID_STOP]) if level == 0 else (ints[OUT_START], ints[OUT_STOP])
        )
        out_at = ints[MID_AT] if level == 0 else ints[OUT_START]
        feat_at = jnp.int32(0) if level == 0 else ints[MID_AT]
        if stage == 0:
            held = refs[4:8]
            copies = [
                pltpu.make_async_copy(source, target, refs[8].at[k])
                for k, (source, target) in enumerate(zip(extras, held))
            ]
            for copy in copies:
                copy.start()
        row8 = lax.broadcasted_iota(jnp.int32, (HEAD, slots), 0)
        scales = [flts[2 * level] * -LOG2E, flts[2 * level + 1]]

        if make_right:
            kind = lax.broadcasted_iota(jnp.int32, (TERMS, 4 * slots), 0)
            lane = lax.broadcasted_iota(jnp.int32, (TERMS, 4 * slots), 1)
            spread = jnp.where(
                jnp.logical_and(kind % HEAD == lane // slots, kind < 3 * HEAD), 1.0, 0.0
            ).astype(jnp.bfloat16)
            for row in range(frame_rows):
                place = home[row, features:tall, :]
                terms = centre_terms(place, float(centre - row), row8, spread)
                for k in range(4):
                    right_ref[row, k] = terms[:, k * slots : (k + 1) * slots]
        if make_near:
            edge = jnp.where(row8 == 3, FAR * FAR, 0.0)
            wheres = views(spec, vals, features, HEAD)
            for c, (_, _, dy, dz, flags) in enumerate(spec):
                near_ref[c, 0] = edge
                near_ref[c, frame_rows + 1] = edge
                gone = jnp.float32(0.0)
                for flag in flags:
                    gone = gone + flts[flag]
                base = jnp.where(row8 == 1, float(dy) * flts[STEP_Y], 0.0)
                base = jnp.where(row8 == 2, float(dz) * flts[STEP_Z], base)
                for row in range(frame_rows):
                    inside = jnp.logical_and(row >= ints[LOW], row < ints[HIGH])
                    lost = gone + jnp.where(inside, 0.0, FAR)
                    near_ref[c, row + 1] = near_terms(
                        wheres[c][row, :, :], base, float(centre - row), lost, row8
                    )
        heads = views(spec, vals, 0, features)

        def pair(turn):
            return [start + 2 * turn, start + 2 * turn + 1]

        turns = (stop - start) // 2
        odd = (stop - start) % 2
        if stage < 2:

            def gather(rows):
                sums = gather_bins(rows, scales, near_ref, heads, right_ref, feat_at)
                for row, total in zip(rows, sums):
                    if prior is not None:
                        total = total + prior[row - out_at]
                    out_ref[row - out_at] = total

            def step(turn, carry):
                gather(pair(turn))
                return carry

            lax.fori_loop(0, turns, step, 0)

            @pl.when(odd == 1)
            def _():
                gather([stop - 1])

            if stage == 0:
                wconv_ref, wup_ref, wupb_ref, wdownb_ref = refs[:4]
                up_ref, upb_ref, downb_ref, conv_in = held
                for copy in copies:
                    copy.wait()
                wconv_ref[...] = jnp.concatenate(
                    [conv_in[level, :, m, :] for m in range(2)], axis=1
                )
                wup_ref[...] = up_ref[level].astype(jnp.float32).T.astype(jnp.bfloat16)
                lift = jnp.broadcast_to(upb_ref[level : level + 1, :], (slots, upb_ref.shape[1])).T
                wupb_ref[...] = jnp.concatenate([lift, lift], axis=1)
                low = jnp.broadcast_to(downb_ref[level : level + 1, :], (slots, features))
                low = jnp.concatenate([low, low], axis=1).T[0:features, :]
                wdownb_ref[...] = jnp.concatenate([low, low], axis=1)

            return

        centre_ref, down_ref, conv_ref, wup_ref, wupb_ref, wdownb_ref = extras
        gath_ref = refs[0]

        def finish(rows, slot):
            size = len(rows) * slots
            packed = gath_ref[slot, :, 0:size]
            mixed = jnp.dot(conv_ref[...], packed, preferred_element_type=jnp.float32)
            centred = mixed - jnp.mean(mixed, axis=0, keepdims=True)
            spread = jnp.mean(centred * centred, axis=0, keepdims=True)
            normed = (centred * lax.rsqrt(spread + EPSILON)).astype(jnp.bfloat16)
            hidden = jnp.dot(wup_ref[...], normed, preferred_element_type=jnp.float32)
            half = 0.5 * (hidden + wupb_ref[:, 0:size])
            hidden = (half + half * jnp.tanh(half)).astype(jnp.bfloat16)
            update = jnp.dot(down_ref[level], hidden, preferred_element_type=jnp.float32)
            update = update + wdownb_ref[:, 0:size]
            for k, row in enumerate(rows):
                source = jnp.clip(row - feat_at, 0, centre_ref.shape[0] - 1)
                kept = centre_ref[source, 0:features, :].astype(jnp.float32)
                far = home[row, features:tall, :].astype(jnp.float32)[3:4, :]
                result = kept + update[:, k * slots : (k + 1) * slots]
                out_ref[row - out_at] = jnp.where(far == 0.0, result, 0.0).astype(jnp.bfloat16)

        for place in range(out_rows):
            out_ref[place] = jnp.zeros((features, slots), jnp.bfloat16)

        def gather(rows, slot, last):
            sums = gather_bins(rows, scales, near_ref, heads, right_ref, feat_at)
            finish(pair(last), 1 - slot)
            both = []
            for row, total in zip(rows, sums):
                total = total + prior[row - out_at]
                both.append(jnp.concatenate([total[:, :slots], total[:, slots:]], axis=0))
            both = both[0] if len(both) == 1 else jnp.concatenate(both, axis=1)
            gath_ref[slot, :, 0 : len(rows) * slots] = both.astype(jnp.bfloat16)

        def step(turn, carry):
            gather(pair(turn), turn % 2, jnp.maximum(turn - 1, 0))
            return carry

        lax.fori_loop(0, turns, step, 0)

        @pl.when(odd == 1)
        def _():
            gather([stop - 1], turns % 2, turns - 1)
            finish([stop - 1], turns % 2)

        @pl.when(odd == 0)
        def _():
            finish(pair(turns - 1), (turns + 1) % 2)

    pairs = out_rows * 3 * len(spec)
    specs = [whole()] * len(inputs)
    scratch = []
    if stage == 0:
        scratch = [pltpu.VMEM(array.shape, array.dtype) for array in extra]
        scratch.append(pltpu.SemaphoreType.DMA((len(extra),)))
        specs[len(inputs) - len(extra) :] = [pl.BlockSpec(memory_space=pltpu.HBM)] * len(extra)
    if stage == 2:
        scratch = [pltpu.VMEM((2, 2 * features, wide), jnp.bfloat16)]
    return pl.pallas_call(
        body,
        out_shape=tuple(outs),
        in_specs=[scalars(), scalars()] + specs,
        out_specs=tuple(whole() for _ in outs),
        scratch_shapes=scratch,
        cost_estimate=pl.CostEstimate(
            flops=pairs * 2 * slots * slots * (2 * features + HEAD),
            transcendentals=pairs * 2 * slots * slots,
            bytes_accessed=pairs * 4 * slots * slots,
        ),
        compiler_params=params(),
    )(ints, flts, *inputs)


def local(
    features,
    positions,
    counts,
    old_cuts,
    new_cuts,
    radial_rates,
    conv_weight,
    up_weight,
    up_bias,
    down_weight,
    down_bias,
):
    peers = lax.axis_size("gx")
    slot_rows = features.shape[0]
    total = peers * slot_rows // 2
    most = min(slot_rows, total - 2 * (peers - 1))
    packed, ints, flts = pack(
        features, positions, counts, old_cuts, new_cuts, radial_rates, most
    )

    if peers == 2:
        other = lax.ppermute(packed, "gx", [(0, 1), (1, 0)])
        frame = assemble(ints, packed, other, total)
        mid_rows = total - 1
    else:
        column = lax.axis_index("gx")
        old_low = old_cuts[column]
        old_high = old_cuts[column + 1]
        held = old_high - old_low
        frame_rows = slot_rows + 4
        base = new_cuts[column] - 2
        pieces = [packed]
        starts = [old_low]
        for by, rows in ((1, 3), (2, 1)):
            tail_at = jnp.maximum(held - rows, 0)
            tail = lax.dynamic_slice_in_dim(packed, tail_at, rows, 0)
            pieces.append(shift(tail, "gx", by))
            back = jnp.maximum(column - by, 0)
            starts.append(jnp.maximum(old_cuts[back], old_cuts[back + 1] - rows))
            pieces.append(shift(packed[:rows], "gx", -by))
            starts.append(old_cuts[jnp.minimum(column + by, peers - 1)])
        layer = base + jnp.arange(frame_rows, dtype=jnp.int32)
        before = old_cuts[jnp.maximum(column - 1, 0)]
        after = old_cuts[jnp.minimum(column + 1, peers - 1) + 1]
        at = []
        first = 0
        for piece, begin in zip(pieces, starts):
            at.append(first + layer - begin)
            first += piece.shape[0]
        choice = jnp.where(
            layer >= old_high,
            jnp.where(layer >= after, at[4], at[2]),
            jnp.where(layer >= old_low, at[0], jnp.where(layer >= before, at[1], at[3])),
        )
        frame = jnp.take(jnp.concatenate(pieces, axis=0), jnp.clip(choice, 0, first - 1), axis=0)
        mid_rows = slot_rows + 2

    own = [(0, None, 0, 0, ())]
    sides = [
        (0, None, -1, 0, (FAR_Y,)),
        (1, None, 1, 0, ()),
        (2, 0, 0, 1, ()),
        (2, 1, -1, 1, (FAR_Y,)),
        (2, 2, 1, 1, ()),
        (3, None, 0, -1, (FAR_Z,)),
    ]
    cross = [
        (0, 0, -1, -1, (FAR_Y, FAR_Z)),
        (0, 1, 1, -1, (FAR_Z,)),
    ]
    up_turned = jnp.transpose(up_weight, (0, 2, 1))

    def layer_of(level, block, known, out_rows):
        up = whole_swap(block, other_y)
        down = partner(block, "gy")
        beyond = whole_swap(block, other_z)
        right, near0, near1, near2 = known
        made = gather_call(
            0,
            level,
            ints,
            flts,
            own,
            frame,
            [block],
            right,
            near0,
            None,
            [outside(array) for array in (up_turned, up_bias, down_bias, conv_weight)],
            out_rows,
        )
        acc, made = made[0], list(made[1:])
        if level == 0:
            right, near0 = made[:2]
        ready = made[-4:]
        acc, up, down, beyond = lax.optimization_barrier((acc, up, down, beyond))
        trio, rims = stacked(block, up, down)
        close = partner(trio, "gz")
        far = whole_swap(rims, other_z)
        made = gather_call(
            1, level, ints, flts, sides, frame, [up, down, close, beyond], right, near1, acc, [], out_rows
        )
        acc = made[0]
        if level == 0:
            near1 = made[1]
        made = gather_call(
            2,
            level,
            ints,
            flts,
            cross,
            frame,
            [far],
            right,
            near2,
            acc,
            [block, down_weight] + ready,
            out_rows,
        )
        if level == 0:
            near2 = made[1]
        return made[0], (right, near0, near1, near2)

    mid, known = layer_of(0, frame, (None,) * 4, mid_rows)
    moved, _ = layer_of(1, mid, known, slot_rows)
    return moved[:, None, None]


def solution(mesh):
    placed = (P("gx", "gy", "gz", None, None),) * 2 + (P("gx", "gy", "gz"),) + (P(),) * 8
    return jax.shard_map(
        local,
        mesh=mesh,
        in_specs=placed,
        out_specs=P("gx", "gy", "gz", None, None),
        check_vma=False,
    )
```

```python
import math

import jax
import jax.numpy as jnp
from jax import lax
from jax.experimental import pallas as pl
from jax.experimental.pallas import tpu as pltpu
from jax.sharding import PartitionSpec as P

EPSILON = 1e-05
FAR = float(2**20)
LOG2E = math.log2(math.e)
HEAD = 8
TERMS = 32
REACH = 3
VMEM_LIMIT = 32 * 2**20

MID_START, MID_STOP, LOW, HIGH, MID_AT, OUT_START, OUT_STOP, CUT, COLUMN = range(9)
STEP_Y, STEP_Z, FAR_Y, FAR_Z = 4, 5, 6, 7


def whole():
    return pl.BlockSpec(memory_space=pltpu.VMEM)


def scalars():
    return pl.BlockSpec(memory_space=pltpu.SMEM)


def outside(array):
    return pltpu.with_memory_space_constraint(array, pltpu.HBM)


def params():
    return pltpu.CompilerParams(vmem_limit_bytes=VMEM_LIMIT)


def shift(block, axis, by):
    count = lax.axis_size(axis)
    return lax.ppermute(block, axis, [(i, (i + by) % count) for i in range(count)])


def partner(block, axis):
    count = lax.axis_size(axis)
    return lax.ppermute(block, axis, [(i, i ^ 1) for i in range(count)])


def whole_swap(block, other):
    axes = ("gx", "gy", "gz")
    sizes = [lax.axis_size(axis) for axis in axes]
    pairs = []
    for gx in range(sizes[0]):
        for gy in range(sizes[1]):
            for gz in range(sizes[2]):
                px, py, pz = other(gx, gy, gz, sizes)
                here = (gx * sizes[1] + gy) * sizes[2] + gz
                pairs.append((here, (px * sizes[1] + py) * sizes[2] + pz))
    return lax.ppermute(block, axes, pairs)


def beside(index):
    return ((index + 1) ^ 1) - 1


def other_y(gx, gy, gz, sizes):
    if 0 < gy < sizes[1] - 1:
        return gx, beside(gy), gz
    return gx, gy, gz ^ 1


def other_z(gx, gy, gz, sizes):
    if 0 < gz < sizes[2] - 1:
        return gx, gy, beside(gz)
    return gx ^ 1, gy, gz


def split3(value):
    first = value.astype(jnp.bfloat16).astype(jnp.float32)
    rest = value - first
    second = rest.astype(jnp.bfloat16).astype(jnp.float32)
    return first, second, rest - second


def pack(features, positions, counts, old_cuts, new_cuts, rates, rows):
    slot_rows, _, _, width, slots = features.shape
    peers = lax.axis_size("gx")
    last_y = lax.axis_size("gy") - 1
    last_z = lax.axis_size("gz") - 1
    total = peers * slot_rows // 2

    def body(
        feat_ref,
        pos_in,
        count_in,
        old_in,
        new_in,
        rate_in,
        out_ref,
        edge_ref,
        int_ref,
        flt_ref,
        pos_ref,
        count_ref,
        old_ref,
        new_ref,
        rate_ref,
        sems,
    ):
        copies = [
            pltpu.make_async_copy(source, target, sems.at[k])
            for k, (source, target) in enumerate(
                (
                    (old_in, old_ref),
                    (new_in, new_ref),
                    (rate_in, rate_ref),
                    (count_in, count_ref),
                    (pos_in, pos_ref),
                    (feat_ref.at[0:rows, 0, 0], out_ref.at[:, 0:width, :]),
                )
            )
        ]
        for copy in copies:
            copy.start()
        for copy in copies[:5]:
            copy.wait()
        column, row_y, row_z = (lax.axis_index(axis) for axis in ("gx", "gy", "gz"))
        new_low, new_high = new_ref[column], new_ref[column + 1]
        if peers == 2:
            base, mid_at = 0, column
        else:
            base, mid_at = new_low - 2, 1
        ints = {
            MID_START: jnp.maximum(new_low - 1, 0) - base,
            MID_STOP: jnp.minimum(new_high + 1, total) - base,
            LOW: jnp.int32(0) - base,
            HIGH: jnp.int32(total) - base,
            MID_AT: jnp.int32(mid_at),
            OUT_START: new_low - base,
            OUT_STOP: new_high - base,
            CUT: old_ref[1],
            COLUMN: column,
        }
        flts = {
            STEP_Y: jnp.where(row_y % 2 == 1, -1.0, 1.0),
            STEP_Z: jnp.where(row_z % 2 == 1, -1.0, 1.0),
            FAR_Y: jnp.where(jnp.logical_or(row_y == 0, row_y == last_y), FAR, 0.0),
            FAR_Z: jnp.where(jnp.logical_or(row_z == 0, row_z == last_z), FAR, 0.0),
        }
        for k in range(2):
            for m in range(2):
                flts[2 * k + m] = rate_ref[k, m]
        lane = lax.broadcasted_iota(jnp.int32, (1, slots), 1)
        line = jnp.zeros((1, slots), jnp.int32)
        for k, value in ints.items():
            line = jnp.where(lane == k, value, line)
        int_ref[...] = line
        line = jnp.zeros((1, slots), jnp.float32)
        for k, value in flts.items():
            line = jnp.where(lane == k, value, line)
        below = jnp.ones((1, slots), jnp.float32)
        for k in range(2):
            below = jnp.where(lane == 2 * k + 1, rate_ref[k, 0], below)
        share = line / below
        flt_ref[...] = share + (line - share * below) / below
        spare = jnp.zeros((HEAD - 4, slots), jnp.float32)
        for row in range(rows):
            place = [pos_ref[d, row : row + 1, :].astype(jnp.float32) for d in range(3)]
            far = jnp.where(lane < count_ref[row], 0.0, FAR)
            block = jnp.concatenate(place + [far, spare], axis=0).astype(jnp.bfloat16)
            out_ref[row, width : width + HEAD, :] = block
        copies[5].wait()
        first = jnp.where(column == 0, jnp.maximum(old_ref[1] - REACH, 0), 0)
        for k in range(REACH):
            edge_ref[k] = out_ref[jnp.minimum(first + k, rows - 1)]

    anywhere = pl.BlockSpec(memory_space=pltpu.HBM)
    return pl.pallas_call(
        body,
        out_shape=(
            jax.ShapeDtypeStruct((rows, width + HEAD, slots), jnp.bfloat16),
            jax.ShapeDtypeStruct((REACH, width + HEAD, slots), jnp.bfloat16),
            jax.ShapeDtypeStruct((1, slots), jnp.int32),
            jax.ShapeDtypeStruct((1, slots), jnp.float32),
        ),
        in_specs=[anywhere] * 6,
        out_specs=(whole(), whole(), whole(), whole()),
        scratch_shapes=[
            pltpu.VMEM((3, slot_rows, slots), positions.dtype),
            pltpu.SMEM((slot_rows,), counts.dtype),
            pltpu.SMEM(old_cuts.shape, old_cuts.dtype),
            pltpu.SMEM(new_cuts.shape, new_cuts.dtype),
            pltpu.SMEM(rates.shape, rates.dtype),
            pltpu.SemaphoreType.DMA((6,)),
        ],
        compiler_params=params(),
    )(
        outside(features),
        outside(jnp.transpose(positions[:, 0, 0], (1, 0, 2))),
        outside(counts.reshape(-1)),
        outside(old_cuts),
        outside(new_cuts),
        outside(rates),
    )


def assemble(ints, mine, other, rows):
    def body(int_ref, mine_ref, other_ref, out_ref):
        cut, column = int_ref[0, CUT], int_ref[0, COLUMN]
        begin = jnp.where(column == 0, cut, jnp.maximum(cut - REACH, 0))
        for row in range(rows):
            owner = (jnp.int32(row) >= cut).astype(jnp.int32)
            place = jnp.clip(row - owner * cut, 0, mine_ref.shape[0] - 1)
            there = jnp.clip(row - begin, 0, REACH - 1)
            out_ref[row] = jnp.where(owner == column, mine_ref[place], other_ref[there])

    return pl.pallas_call(
        body,
        out_shape=jax.ShapeDtypeStruct((rows,) + mine.shape[1:], mine.dtype),
        in_specs=[scalars(), whole(), whole()],
        out_specs=whole(),
        compiler_params=params(),
    )(ints, mine, other)


def stacked(block, up, down):
    def body(block_ref, up_ref, down_ref, trio_ref, rims_ref):
        for row in range(block.shape[0]):
            trio_ref[0, row] = block_ref[row]
            for k, ref in enumerate((up_ref, down_ref)):
                value = ref[row]
                trio_ref[k + 1, row] = value
                rims_ref[k, row] = value

    return pl.pallas_call(
        body,
        out_shape=tuple(
            jax.ShapeDtypeStruct((count,) + block.shape, block.dtype) for count in (3, 2)
        ),
        in_specs=[whole()] * 3,
        out_specs=(whole(), whole()),
        compiler_params=params(),
    )(block, up, down)


def centre_terms(place, along, row8, spread):
    here = place.astype(jnp.float32)
    live = row8 < 3
    at = jnp.where(row8 == 0, here + along, jnp.where(live, here, 0.0))
    norm = jnp.sum(at * at, axis=0, keepdims=True)
    rows = jnp.where(row8 == 3, norm, -2.0 * at)
    stack = jnp.concatenate(split3(rows) + (jnp.zeros_like(rows),), axis=0)
    return jnp.dot(stack.T.astype(jnp.bfloat16), spread, preferred_element_type=jnp.float32)


def near_terms(place, base, along, gone, row8):
    there = place.astype(jnp.float32)
    far = there[3:4, :] + gone
    at = jnp.where(row8 == 0, there + along, jnp.where(row8 < 3, there - base, 0.0))
    norm = jnp.sum(at * at, axis=0, keepdims=True)
    norm = jnp.where(far > 0.0, FAR * FAR, norm)
    return jnp.where(row8 == 3, norm, at)


def gather_bins(rows, scales, near_ref, feats, centre_ref, feat_at):
    sums = []
    scale, ratio = scales
    for row in rows:
        minus = [centre_ref[row, k] for k in range(3)]
        norm = centre_ref[row, 3] * scale
        items = [(c, dx) for c in range(len(feats)) for dx in range(3)]
        total = None
        for k in range(0, len(items), 2):
            weights = [[], []]
            vals = []
            for c, dx in items[k : k + 2]:
                near = near_ref[c, row + dx] * scale
                power = norm + near[3:4, :]
                for d in range(3):
                    power = power + minus[d] * near[d : d + 1, :]
                weights[0].append(jnp.exp2(power).astype(jnp.bfloat16))
                weights[1].append(jnp.exp2(power * ratio).astype(jnp.bfloat16))
                source = jnp.clip(row + dx - 1 - feat_at, 0, feats[c].shape[0] - 1)
                vals.append(feats[c][source, :, :])
            if len(vals) == 1:
                feat = vals[0]
                sides = [group[0] for group in weights]
            else:
                feat = jnp.concatenate(vals, axis=1)
                sides = [jnp.concatenate(group, axis=1) for group in weights]
            part = lax.dot_general(
                feat,
                jnp.concatenate(sides, axis=0),
                (((1,), (1,)), ((), ())),
                preferred_element_type=jnp.float32,
            )
            total = part if total is None else total + part
        sums.append(total)
    return sums


def views(spec, arrays, start, size):
    found = []
    for index, sub, *_ in spec:
        ref = arrays[index] if sub is None else arrays[index].at[sub]
        found.append(ref.at[:, start : start + size, :])
    return found


def gather_call(stage, level, ints, flts, spec, frame, feats, right, near, before, extra, out_rows):
    frame_rows, tall, slots = frame.shape
    features = tall - HEAD
    centre = frame_rows // 2
    make_right = right is None
    make_near = near is None
    inputs = [frame] + list(feats)
    if not make_right:
        inputs.append(right)
    if not make_near:
        inputs.append(near)
    if before is not None:
        inputs.append(before)
    inputs += list(extra)
    outs = []
    wide = 2 * slots
    if stage < 2:
        outs.append(jax.ShapeDtypeStruct((out_rows, features, wide), jnp.float32))
    else:
        outs.append(jax.ShapeDtypeStruct((out_rows, features, slots), jnp.bfloat16))
    if make_right:
        outs.append(jax.ShapeDtypeStruct((frame_rows, 4, slots, slots), jnp.float32))
    if make_near:
        outs.append(
            jax.ShapeDtypeStruct((len(spec), frame_rows + 2, HEAD, slots), jnp.float32)
        )
    if stage == 0:
        hid = extra[0].shape[2]
        outs.append(jax.ShapeDtypeStruct((features, 2 * features), jnp.bfloat16))
        outs.append(jax.ShapeDtypeStruct((hid, features), jnp.bfloat16))
        outs.append(jax.ShapeDtypeStruct((hid, wide), jnp.float32))
        outs.append(jax.ShapeDtypeStruct((features, wide), jnp.float32))

    def body(*refs):
        refs = list(refs)
        ints, flts = refs.pop(0).at[0], refs.pop(0).at[0]
        home = refs.pop(0)
        vals = [refs.pop(0) for _ in feats]
        right_ref = None if make_right else refs.pop(0)
        near_ref = None if make_near else refs.pop(0)
        prior = None if before is None else refs.pop(0)
        extras = [refs.pop(0) for _ in extra]
        out_ref = refs.pop(0)
        right_ref = refs.pop(0) if make_right else right_ref
        near_ref = refs.pop(0) if make_near else near_ref
        start, stop = (
            (ints[MID_START], ints[MID_STOP]) if level == 0 else (ints[OUT_START], ints[OUT_STOP])
        )
        out_at = ints[MID_AT] if level == 0 else ints[OUT_START]
        feat_at = jnp.int32(0) if level == 0 else ints[MID_AT]
        if stage == 0:
            held = refs[4:8]
            copies = [
                pltpu.make_async_copy(source, target, refs[8].at[k])
                for k, (source, target) in enumerate(zip(extras, held))
            ]
            for copy in copies:
                copy.start()
        row8 = lax.broadcasted_iota(jnp.int32, (HEAD, slots), 0)
        scales = [flts[2 * level] * -LOG2E, flts[2 * level + 1]]

        if make_right:
            kind = lax.broadcasted_iota(jnp.int32, (TERMS, 4 * slots), 0)
            lane = lax.broadcasted_iota(jnp.int32, (TERMS, 4 * slots), 1)
            spread = jnp.where(
                jnp.logical_and(kind % HEAD == lane // slots, kind < 3 * HEAD), 1.0, 0.0
            ).astype(jnp.bfloat16)
            for row in range(frame_rows):
                place = home[row, features:tall, :]
                terms = centre_terms(place, float(centre - row), row8, spread)
                for k in range(4):
                    right_ref[row, k] = terms[:, k * slots : (k + 1) * slots]
        if make_near:
            edge = jnp.where(row8 == 3, FAR * FAR, 0.0)
            wheres = views(spec, vals, features, HEAD)
            for c, (_, _, dy, dz, flags) in enumerate(spec):
                near_ref[c, 0] = edge
                near_ref[c, frame_rows + 1] = edge
                gone = jnp.float32(0.0)
                for flag in flags:
                    gone = gone + flts[flag]
                base = jnp.where(row8 == 1, float(dy) * flts[STEP_Y], 0.0)
                base = jnp.where(row8 == 2, float(dz) * flts[STEP_Z], base)
                for row in range(frame_rows):
                    inside = jnp.logical_and(row >= ints[LOW], row < ints[HIGH])
                    lost = gone + jnp.where(inside, 0.0, FAR)
                    near_ref[c, row + 1] = near_terms(
                        wheres[c][row, :, :], base, float(centre - row), lost, row8
                    )
        heads = views(spec, vals, 0, features)

        def pair(turn):
            return [start + 2 * turn, start + 2 * turn + 1]

        turns = (stop - start) // 2
        odd = (stop - start) % 2
        if stage < 2:

            def gather(rows):
                sums = gather_bins(rows, scales, near_ref, heads, right_ref, feat_at)
                for row, total in zip(rows, sums):
                    if prior is not None:
                        total = total + prior[row - out_at]
                    out_ref[row - out_at] = total

            def step(turn, carry):
                gather(pair(turn))
                return carry

            lax.fori_loop(0, turns, step, 0)

            @pl.when(odd == 1)
            def _():
                gather([stop - 1])

            if stage == 0:
                wconv_ref, wup_ref, wupb_ref, wdownb_ref = refs[:4]
                up_ref, upb_ref, downb_ref, conv_in = held
                for copy in copies:
                    copy.wait()
                wconv_ref[...] = jnp.concatenate(
                    [conv_in[level, :, m, :] for m in range(2)], axis=1
                )
                wup_ref[...] = (0.5 * up_ref[level].astype(jnp.float32)).T.astype(jnp.bfloat16)
                lift = 0.5 * jnp.broadcast_to(upb_ref[level : level + 1, :], (slots, upb_ref.shape[1])).T
                wupb_ref[...] = jnp.concatenate([lift, lift], axis=1)
                low = jnp.broadcast_to(downb_ref[level : level + 1, :], (slots, features))
                low = jnp.concatenate([low, low], axis=1).T[0:features, :]
                wdownb_ref[...] = jnp.concatenate([low, low], axis=1)

            return

        centre_ref, down_ref, conv_ref, wup_ref, wupb_ref, wdownb_ref = extras
        gath_ref = refs[0]

        def finish(rows, slot):
            size = len(rows) * slots
            packed = gath_ref[slot, :, 0:size]
            mixed = jnp.dot(conv_ref[...], packed, preferred_element_type=jnp.float32)
            centred = mixed - jnp.mean(mixed, axis=0, keepdims=True)
            spread = jnp.mean(centred * centred, axis=0, keepdims=True)
            normed = (centred * lax.rsqrt(spread + EPSILON)).astype(jnp.bfloat16)
            hidden = jnp.dot(wup_ref[...], normed, preferred_element_type=jnp.float32)
            half = hidden + wupb_ref[:, 0:size]
            hidden = (half + half * jnp.tanh(half)).astype(jnp.bfloat16)
            update = jnp.dot(down_ref[level], hidden, preferred_element_type=jnp.float32)
            update = update + wdownb_ref[:, 0:size]
            for k, row in enumerate(rows):
                source = jnp.clip(row - feat_at, 0, centre_ref.shape[0] - 1)
                kept = centre_ref[source, 0:features, :].astype(jnp.float32)
                far = home[row, features:tall, :].astype(jnp.float32)[3:4, :]
                result = kept + update[:, k * slots : (k + 1) * slots]
                out_ref[row - out_at] = jnp.where(far == 0.0, result, 0.0).astype(jnp.bfloat16)

        for place in range(out_rows):
            out_ref[place] = jnp.zeros((features, slots), jnp.bfloat16)

        def gather(rows, slot, last):
            sums = gather_bins(rows, scales, near_ref, heads, right_ref, feat_at)
            finish(pair(last), 1 - slot)
            both = []
            for row, total in zip(rows, sums):
                total = total + prior[row - out_at]
                both.append(jnp.concatenate([total[:, :slots], total[:, slots:]], axis=0))
            both = both[0] if len(both) == 1 else jnp.concatenate(both, axis=1)
            gath_ref[slot, :, 0 : len(rows) * slots] = both.astype(jnp.bfloat16)

        def step(turn, carry):
            gather(pair(turn), turn % 2, jnp.maximum(turn - 1, 0))
            return carry

        lax.fori_loop(0, turns, step, 0)

        @pl.when(odd == 1)
        def _():
            gather([stop - 1], turns % 2, turns - 1)
            finish([stop - 1], turns % 2)

        @pl.when(odd == 0)
        def _():
            finish(pair(turns - 1), (turns + 1) % 2)

    pairs = out_rows * 3 * len(spec)
    specs = [whole()] * len(inputs)
    scratch = []
    if stage == 0:
        scratch = [pltpu.VMEM(array.shape, array.dtype) for array in extra]
        scratch.append(pltpu.SemaphoreType.DMA((len(extra),)))
        specs[len(inputs) - len(extra) :] = [pl.BlockSpec(memory_space=pltpu.HBM)] * len(extra)
    if stage == 2:
        scratch = [pltpu.VMEM((2, 2 * features, wide), jnp.bfloat16)]
    return pl.pallas_call(
        body,
        out_shape=tuple(outs),
        in_specs=[scalars(), scalars()] + specs,
        out_specs=tuple(whole() for _ in outs),
        scratch_shapes=scratch,
        cost_estimate=pl.CostEstimate(
            flops=pairs * 2 * slots * slots * (2 * features + HEAD),
            transcendentals=pairs * 2 * slots * slots,
            bytes_accessed=pairs * 4 * slots * slots,
        ),
        compiler_params=params(),
    )(ints, flts, *inputs)


def local(
    features,
    positions,
    counts,
    old_cuts,
    new_cuts,
    radial_rates,
    conv_weight,
    up_weight,
    up_bias,
    down_weight,
    down_bias,
):
    peers = lax.axis_size("gx")
    slot_rows = features.shape[0]
    total = peers * slot_rows // 2
    most = min(slot_rows, total - 2 * (peers - 1))
    packed, edge, ints, flts = pack(
        features, positions, counts, old_cuts, new_cuts, radial_rates, most
    )

    if peers == 2:
        other = lax.ppermute(edge, "gx", [(0, 1), (1, 0)])
        frame = assemble(ints, packed, other, total)
        mid_rows = total - 1
    else:
        column = lax.axis_index("gx")
        old_low = old_cuts[column]
        old_high = old_cuts[column + 1]
        held = old_high - old_low
        frame_rows = slot_rows + 4
        base = new_cuts[column] - 2
        pieces = [packed]
        starts = [old_low]
        for by, rows in ((1, REACH), (2, 1)):
            tail_at = jnp.maximum(held - rows, 0)
            tail = lax.dynamic_slice_in_dim(packed, tail_at, rows, 0)
            pieces.append(shift(tail, "gx", by))
            back = jnp.maximum(column - by, 0)
            starts.append(jnp.maximum(old_cuts[back], old_cuts[back + 1] - rows))
            pieces.append(shift(packed[:rows], "gx", -by))
            starts.append(old_cuts[jnp.minimum(column + by, peers - 1)])
        layer = base + jnp.arange(frame_rows, dtype=jnp.int32)
        before = old_cuts[jnp.maximum(column - 1, 0)]
        after = old_cuts[jnp.minimum(column + 1, peers - 1) + 1]
        at = []
        first = 0
        for piece, begin in zip(pieces, starts):
            at.append(first + layer - begin)
            first += piece.shape[0]
        choice = jnp.where(
            layer >= old_high,
            jnp.where(layer >= after, at[4], at[2]),
            jnp.where(layer >= old_low, at[0], jnp.where(layer >= before, at[1], at[3])),
        )
        frame = jnp.take(jnp.concatenate(pieces, axis=0), jnp.clip(choice, 0, first - 1), axis=0)
        mid_rows = slot_rows + 2

    own = [(0, None, 0, 0, ())]
    sides = [
        (0, None, -1, 0, (FAR_Y,)),
        (1, None, 1, 0, ()),
        (2, 0, 0, 1, ()),
        (2, 1, -1, 1, (FAR_Y,)),
        (2, 2, 1, 1, ()),
        (3, None, 0, -1, (FAR_Z,)),
    ]
    cross = [
        (0, 0, -1, -1, (FAR_Y, FAR_Z)),
        (0, 1, 1, -1, (FAR_Z,)),
    ]
    up_turned = jnp.transpose(up_weight, (0, 2, 1))

    def layer_of(level, block, known, out_rows):
        up = whole_swap(block, other_y)
        down = partner(block, "gy")
        beyond = whole_swap(block, other_z)
        right, near0, near1, near2 = known
        made = gather_call(
            0,
            level,
            ints,
            flts,
            own,
            frame,
            [block],
            right,
            near0,
            None,
            [outside(array) for array in (up_turned, up_bias, down_bias, conv_weight)],
            out_rows,
        )
        acc, made = made[0], list(made[1:])
        if level == 0:
            right, near0 = made[:2]
        ready = made[-4:]
        acc, up, down, beyond = lax.optimization_barrier((acc, up, down, beyond))
        trio, rims = stacked(block, up, down)
        close = partner(trio, "gz")
        far = whole_swap(rims, other_z)
        made = gather_call(
            1, level, ints, flts, sides, frame, [up, down, close, beyond], right, near1, acc, [], out_rows
        )
        acc = made[0]
        if level == 0:
            near1 = made[1]
        made = gather_call(
            2,
            level,
            ints,
            flts,
            cross,
            frame,
            [far],
            right,
            near2,
            acc,
            [block, down_weight] + ready,
            out_rows,
        )
        if level == 0:
            near2 = made[1]
        return made[0], (right, near0, near1, near2)

    mid, known = layer_of(0, frame, (None,) * 4, mid_rows)
    moved, _ = layer_of(1, mid, known, slot_rows)
    return moved[:, None, None]


def solution(mesh):
    placed = (P("gx", "gy", "gz", None, None),) * 2 + (P("gx", "gy", "gz"),) + (P(),) * 8
    return jax.shard_map(
        local,
        mesh=mesh,
        in_specs=placed,
        out_specs=P("gx", "gy", "gz", None, None),
        check_vma=False,
    )
```

```python
import math

import jax
import jax.numpy as jnp
from jax import lax
from jax.experimental import pallas as pl
from jax.experimental.pallas import tpu as pltpu
from jax.sharding import PartitionSpec as P

EPSILON = 1e-05
FAR = float(2**20)
LOG2E = math.log2(math.e)
HEAD = 8
TERMS = 32
REACH = 3
VMEM_LIMIT = 32 * 2**20

MID_START, MID_STOP, LOW, HIGH, MID_AT, OUT_START, OUT_STOP, CUT, COLUMN = range(9)
STEP_Y, STEP_Z, FAR_Y, FAR_Z = 4, 5, 6, 7


def whole():
    return pl.BlockSpec(memory_space=pltpu.VMEM)


def scalars():
    return pl.BlockSpec(memory_space=pltpu.SMEM)


def outside(array):
    return pltpu.with_memory_space_constraint(array, pltpu.HBM)


def params():
    return pltpu.CompilerParams(vmem_limit_bytes=VMEM_LIMIT)


def shift(block, axis, by):
    count = lax.axis_size(axis)
    return lax.ppermute(block, axis, [(i, (i + by) % count) for i in range(count)])


def partner(block, axis):
    count = lax.axis_size(axis)
    return lax.ppermute(block, axis, [(i, i ^ 1) for i in range(count)])


def whole_swap(block, other):
    axes = ("gx", "gy", "gz")
    sizes = [lax.axis_size(axis) for axis in axes]
    pairs = []
    for gx in range(sizes[0]):
        for gy in range(sizes[1]):
            for gz in range(sizes[2]):
                px, py, pz = other(gx, gy, gz, sizes)
                here = (gx * sizes[1] + gy) * sizes[2] + gz
                pairs.append((here, (px * sizes[1] + py) * sizes[2] + pz))
    return lax.ppermute(block, axes, pairs)


def beside(index):
    return ((index + 1) ^ 1) - 1


def other_y(gx, gy, gz, sizes):
    if 0 < gy < sizes[1] - 1:
        return gx, beside(gy), gz
    return gx, gy, gz ^ 1


def other_z(gx, gy, gz, sizes):
    if 0 < gz < sizes[2] - 1:
        return gx, gy, beside(gz)
    return gx ^ 1, gy, gz


def split3(value):
    first = value.astype(jnp.bfloat16).astype(jnp.float32)
    rest = value - first
    second = rest.astype(jnp.bfloat16).astype(jnp.float32)
    return first, second, rest - second


def pack(features, positions, counts, old_cuts, new_cuts, rates, rows):
    slot_rows, _, _, width, slots = features.shape
    peers = lax.axis_size("gx")
    last_y = lax.axis_size("gy") - 1
    last_z = lax.axis_size("gz") - 1
    total = peers * slot_rows // 2

    def body(
        feat_ref,
        pos_in,
        count_in,
        old_in,
        new_in,
        rate_in,
        out_ref,
        edge_ref,
        int_ref,
        flt_ref,
        pos_ref,
        count_ref,
        old_ref,
        new_ref,
        rate_ref,
        sems,
    ):
        copies = [
            pltpu.make_async_copy(source, target, sems.at[k])
            for k, (source, target) in enumerate(
                (
                    (old_in, old_ref),
                    (new_in, new_ref),
                    (rate_in, rate_ref),
                    (count_in, count_ref),
                    (pos_in, pos_ref),
                    (feat_ref.at[0:rows, 0, 0], out_ref.at[:, 0:width, :]),
                )
            )
        ]
        for copy in copies:
            copy.start()
        for copy in copies[:5]:
            copy.wait()
        column, row_y, row_z = (lax.axis_index(axis) for axis in ("gx", "gy", "gz"))
        new_low, new_high = new_ref[column], new_ref[column + 1]
        if peers == 2:
            base, mid_at = 0, column
        else:
            base, mid_at = new_low - 2, 1
        ints = {
            MID_START: jnp.maximum(new_low - 1, 0) - base,
            MID_STOP: jnp.minimum(new_high + 1, total) - base,
            LOW: jnp.int32(0) - base,
            HIGH: jnp.int32(total) - base,
            MID_AT: jnp.int32(mid_at),
            OUT_START: new_low - base,
            OUT_STOP: new_high - base,
            CUT: old_ref[1],
            COLUMN: column,
        }
        flts = {
            STEP_Y: jnp.where(row_y % 2 == 1, -1.0, 1.0),
            STEP_Z: jnp.where(row_z % 2 == 1, -1.0, 1.0),
            FAR_Y: jnp.where(jnp.logical_or(row_y == 0, row_y == last_y), FAR, 0.0),
            FAR_Z: jnp.where(jnp.logical_or(row_z == 0, row_z == last_z), FAR, 0.0),
        }
        for k in range(2):
            for m in range(2):
                flts[2 * k + m] = rate_ref[k, m]
        lane = lax.broadcasted_iota(jnp.int32, (1, slots), 1)
        line = jnp.zeros((1, slots), jnp.int32)
        for k, value in ints.items():
            line = jnp.where(lane == k, value, line)
        int_ref[...] = line
        line = jnp.zeros((1, slots), jnp.float32)
        for k, value in flts.items():
            line = jnp.where(lane == k, value, line)
        below = jnp.ones((1, slots), jnp.float32)
        for k in range(2):
            below = jnp.where(lane == 2 * k + 1, rate_ref[k, 0], below)
        share = line / below
        flt_ref[...] = share + (line - share * below) / below
        spare = jnp.zeros((HEAD - 4, slots), jnp.float32)
        for row in range(rows):
            place = [pos_ref[d, row : row + 1, :].astype(jnp.float32) for d in range(3)]
            far = jnp.where(lane < count_ref[row], 0.0, FAR)
            block = jnp.concatenate(place + [far, spare], axis=0).astype(jnp.bfloat16)
            out_ref[row, width : width + HEAD, :] = block
        copies[5].wait()
        first = jnp.where(column == 0, jnp.maximum(old_ref[1] - REACH, 0), 0)
        for k in range(REACH):
            edge_ref[k] = out_ref[jnp.minimum(first + k, rows - 1)]

    anywhere = pl.BlockSpec(memory_space=pltpu.HBM)
    return pl.pallas_call(
        body,
        out_shape=(
            jax.ShapeDtypeStruct((rows, width + HEAD, slots), jnp.bfloat16),
            jax.ShapeDtypeStruct((REACH, width + HEAD, slots), jnp.bfloat16),
            jax.ShapeDtypeStruct((1, slots), jnp.int32),
            jax.ShapeDtypeStruct((1, slots), jnp.float32),
        ),
        in_specs=[anywhere] * 6,
        out_specs=(whole(), whole(), whole(), whole()),
        scratch_shapes=[
            pltpu.VMEM((3, slot_rows, slots), positions.dtype),
            pltpu.SMEM((slot_rows,), counts.dtype),
            pltpu.SMEM(old_cuts.shape, old_cuts.dtype),
            pltpu.SMEM(new_cuts.shape, new_cuts.dtype),
            pltpu.SMEM(rates.shape, rates.dtype),
            pltpu.SemaphoreType.DMA((6,)),
        ],
        compiler_params=params(),
    )(
        outside(features),
        outside(jnp.transpose(positions[:, 0, 0], (1, 0, 2))),
        outside(counts.reshape(-1)),
        outside(old_cuts),
        outside(new_cuts),
        outside(rates),
    )


def assemble(ints, mine, other, rows):
    def body(int_ref, mine_ref, other_ref, out_ref):
        cut, column = int_ref[0, CUT], int_ref[0, COLUMN]
        begin = jnp.where(column == 0, cut, jnp.maximum(cut - REACH, 0))
        for row in range(rows):
            owner = (jnp.int32(row) >= cut).astype(jnp.int32)
            place = jnp.clip(row - owner * cut, 0, mine_ref.shape[0] - 1)
            there = jnp.clip(row - begin, 0, REACH - 1)
            out_ref[row] = jnp.where(owner == column, mine_ref[place], other_ref[there])

    return pl.pallas_call(
        body,
        out_shape=jax.ShapeDtypeStruct((rows,) + mine.shape[1:], mine.dtype),
        in_specs=[scalars(), whole(), whole()],
        out_specs=whole(),
        compiler_params=params(),
    )(ints, mine, other)


def stacked(block, up, down):
    def body(block_ref, up_ref, down_ref, trio_ref, rims_ref):
        for row in range(block.shape[0]):
            trio_ref[0, row] = block_ref[row]
            for k, ref in enumerate((up_ref, down_ref)):
                value = ref[row]
                trio_ref[k + 1, row] = value
                rims_ref[k, row] = value

    return pl.pallas_call(
        body,
        out_shape=tuple(
            jax.ShapeDtypeStruct((count,) + block.shape, block.dtype) for count in (3, 2)
        ),
        in_specs=[whole()] * 3,
        out_specs=(whole(), whole()),
        compiler_params=params(),
    )(block, up, down)


def centre_terms(place, along, row8, spread):
    here = place.astype(jnp.float32)
    live = row8 < 3
    at = jnp.where(row8 == 0, here + along, jnp.where(live, here, 0.0))
    norm = jnp.sum(at * at, axis=0, keepdims=True)
    rows = jnp.where(row8 == 3, norm, -2.0 * at)
    stack = jnp.concatenate(split3(rows) + (jnp.zeros_like(rows),), axis=0)
    return jnp.dot(stack.T.astype(jnp.bfloat16), spread, preferred_element_type=jnp.float32)


def near_terms(place, base, along, gone, row8):
    there = place.astype(jnp.float32)
    far = there[3:4, :] + gone
    at = jnp.where(row8 == 0, there + along, jnp.where(row8 < 3, there - base, 0.0))
    norm = jnp.sum(at * at, axis=0, keepdims=True)
    norm = jnp.where(far > 0.0, FAR * FAR, norm)
    return jnp.where(row8 == 3, norm, at)


def gather_bins(rows, scales, near_ref, feats, centre_ref, feat_at):
    sums = []
    scale, ratio = scales
    for row in rows:
        minus = [centre_ref[row, k] for k in range(3)]
        norm = centre_ref[row, 3] * scale
        items = [(c, dx) for c in range(len(feats)) for dx in range(3)]
        total = None
        for k in range(0, len(items), 6):
            weights = [[], []]
            vals = []
            for c, dx in items[k : k + 6]:
                near = near_ref[c, row + dx] * scale
                power = norm + near[3:4, :]
                for d in range(3):
                    power = power + minus[d] * near[d : d + 1, :]
                weights[0].append(jnp.exp2(power).astype(jnp.bfloat16))
                weights[1].append(jnp.exp2(power * ratio).astype(jnp.bfloat16))
                source = jnp.clip(row + dx - 1 - feat_at, 0, feats[c].shape[0] - 1)
                vals.append(feats[c][source, :, :])
            if len(vals) == 1:
                feat = vals[0]
                sides = [group[0] for group in weights]
            else:
                feat = jnp.concatenate(vals, axis=1)
                sides = [jnp.concatenate(group, axis=1) for group in weights]
            part = lax.dot_general(
                feat,
                jnp.concatenate(sides, axis=0),
                (((1,), (1,)), ((), ())),
                preferred_element_type=jnp.float32,
            )
            total = part if total is None else total + part
        sums.append(total)
    return sums


def views(spec, arrays, start, size):
    found = []
    for index, sub, *_ in spec:
        ref = arrays[index] if sub is None else arrays[index].at[sub]
        found.append(ref.at[:, start : start + size, :])
    return found


def gather_call(stage, level, ints, flts, spec, frame, feats, right, near, before, extra, out_rows):
    frame_rows, tall, slots = frame.shape
    features = tall - HEAD
    centre = frame_rows // 2
    make_right = right is None
    make_near = near is None
    inputs = [frame] + list(feats)
    if not make_right:
        inputs.append(right)
    if not make_near:
        inputs.append(near)
    if before is not None:
        inputs.append(before)
    inputs += list(extra)
    outs = []
    wide = 2 * slots
    if stage < 2:
        outs.append(jax.ShapeDtypeStruct((out_rows, features, wide), jnp.float32))
    else:
        outs.append(jax.ShapeDtypeStruct((out_rows, features, slots), jnp.bfloat16))
    if make_right:
        outs.append(jax.ShapeDtypeStruct((frame_rows, 4, slots, slots), jnp.float32))
    if make_near:
        outs.append(
            jax.ShapeDtypeStruct((len(spec), frame_rows + 2, HEAD, slots), jnp.float32)
        )
    if stage == 0:
        hid = extra[0].shape[2]
        outs.append(jax.ShapeDtypeStruct((features, 2 * features), jnp.bfloat16))
        outs.append(jax.ShapeDtypeStruct((hid, features), jnp.bfloat16))
        outs.append(jax.ShapeDtypeStruct((hid, wide), jnp.float32))
        outs.append(jax.ShapeDtypeStruct((features, wide), jnp.float32))

    def body(*refs):
        refs = list(refs)
        ints, flts = refs.pop(0).at[0], refs.pop(0).at[0]
        home = refs.pop(0)
        vals = [refs.pop(0) for _ in feats]
        right_ref = None if make_right else refs.pop(0)
        near_ref = None if make_near else refs.pop(0)
        prior = None if before is None else refs.pop(0)
        extras = [refs.pop(0) for _ in extra]
        out_ref = refs.pop(0)
        right_ref = refs.pop(0) if make_right else right_ref
        near_ref = refs.pop(0) if make_near else near_ref
        start, stop = (
            (ints[MID_START], ints[MID_STOP]) if level == 0 else (ints[OUT_START], ints[OUT_STOP])
        )
        out_at = ints[MID_AT] if level == 0 else ints[OUT_START]
        feat_at = jnp.int32(0) if level == 0 else ints[MID_AT]
        if stage == 0:
            held = refs[4:8]
            copies = [
                pltpu.make_async_copy(source, target, refs[8].at[k])
                for k, (source, target) in enumerate(zip(extras, held))
            ]
            for copy in copies:
                copy.start()
        row8 = lax.broadcasted_iota(jnp.int32, (HEAD, slots), 0)
        scales = [flts[2 * level] * -LOG2E, flts[2 * level + 1]]

        if make_right:
            kind = lax.broadcasted_iota(jnp.int32, (TERMS, 4 * slots), 0)
            lane = lax.broadcasted_iota(jnp.int32, (TERMS, 4 * slots), 1)
            spread = jnp.where(
                jnp.logical_and(kind % HEAD == lane // slots, kind < 3 * HEAD), 1.0, 0.0
            ).astype(jnp.bfloat16)
            for row in range(frame_rows):
                place = home[row, features:tall, :]
                terms = centre_terms(place, float(centre - row), row8, spread)
                for k in range(4):
                    right_ref[row, k] = terms[:, k * slots : (k + 1) * slots]
        if make_near:
            edge = jnp.where(row8 == 3, FAR * FAR, 0.0)
            wheres = views(spec, vals, features, HEAD)
            for c, (_, _, dy, dz, flags) in enumerate(spec):
                near_ref[c, 0] = edge
                near_ref[c, frame_rows + 1] = edge
                gone = jnp.float32(0.0)
                for flag in flags:
                    gone = gone + flts[flag]
                base = jnp.where(row8 == 1, float(dy) * flts[STEP_Y], 0.0)
                base = jnp.where(row8 == 2, float(dz) * flts[STEP_Z], base)
                for row in range(frame_rows):
                    inside = jnp.logical_and(row >= ints[LOW], row < ints[HIGH])
                    lost = gone + jnp.where(inside, 0.0, FAR)
                    near_ref[c, row + 1] = near_terms(
                        wheres[c][row, :, :], base, float(centre - row), lost, row8
                    )
        heads = views(spec, vals, 0, features)

        def pair(turn):
            return [start + 2 * turn, start + 2 * turn + 1]

        turns = (stop - start) // 2
        odd = (stop - start) % 2
        if stage < 2:

            def gather(rows):
                sums = gather_bins(rows, scales, near_ref, heads, right_ref, feat_at)
                for row, total in zip(rows, sums):
                    if prior is not None:
                        total = total + prior[row - out_at]
                    out_ref[row - out_at] = total

            def step(turn, carry):
                gather(pair(turn))
                return carry

            lax.fori_loop(0, turns, step, 0)

            @pl.when(odd == 1)
            def _():
                gather([stop - 1])

            if stage == 0:
                wconv_ref, wup_ref, wupb_ref, wdownb_ref = refs[:4]
                up_ref, upb_ref, downb_ref, conv_in = held
                for copy in copies:
                    copy.wait()
                wconv_ref[...] = jnp.concatenate(
                    [conv_in[level, :, m, :] for m in range(2)], axis=1
                )
                wup_ref[...] = (0.5 * up_ref[level].astype(jnp.float32)).T.astype(jnp.bfloat16)
                lift = 0.5 * jnp.broadcast_to(upb_ref[level : level + 1, :], (slots, upb_ref.shape[1])).T
                wupb_ref[...] = jnp.concatenate([lift, lift], axis=1)
                low = jnp.broadcast_to(downb_ref[level : level + 1, :], (slots, features))
                low = jnp.concatenate([low, low], axis=1).T[0:features, :]
                wdownb_ref[...] = jnp.concatenate([low, low], axis=1)

            return

        centre_ref, down_ref, conv_ref, wup_ref, wupb_ref, wdownb_ref = extras
        gath_ref = refs[0]

        def finish(rows, slot):
            size = len(rows) * slots
            packed = gath_ref[slot, :, 0:size]
            mixed = jnp.dot(conv_ref[...], packed, preferred_element_type=jnp.float32)
            centred = mixed - jnp.mean(mixed, axis=0, keepdims=True)
            spread = jnp.mean(centred * centred, axis=0, keepdims=True)
            normed = (centred * lax.rsqrt(spread + EPSILON)).astype(jnp.bfloat16)
            hidden = jnp.dot(wup_ref[...], normed, preferred_element_type=jnp.float32)
            half = hidden + wupb_ref[:, 0:size]
            hidden = (half + half * jnp.tanh(half)).astype(jnp.bfloat16)
            update = jnp.dot(down_ref[level], hidden, preferred_element_type=jnp.float32)
            update = update + wdownb_ref[:, 0:size]
            for k, row in enumerate(rows):
                source = jnp.clip(row - feat_at, 0, centre_ref.shape[0] - 1)
                kept = centre_ref[source, 0:features, :].astype(jnp.float32)
                far = home[row, features:tall, :].astype(jnp.float32)[3:4, :]
                result = kept + update[:, k * slots : (k + 1) * slots]
                out_ref[row - out_at] = jnp.where(far == 0.0, result, 0.0).astype(jnp.bfloat16)

        for place in range(out_rows):
            out_ref[place] = jnp.zeros((features, slots), jnp.bfloat16)

        def gather(rows, slot, last):
            sums = gather_bins(rows, scales, near_ref, heads, right_ref, feat_at)
            finish(pair(last), 1 - slot)
            both = []
            for row, total in zip(rows, sums):
                total = total + prior[row - out_at]
                both.append(jnp.concatenate([total[:, :slots], total[:, slots:]], axis=0))
            both = both[0] if len(both) == 1 else jnp.concatenate(both, axis=1)
            gath_ref[slot, :, 0 : len(rows) * slots] = both.astype(jnp.bfloat16)

        def step(turn, carry):
            gather(pair(turn), turn % 2, jnp.maximum(turn - 1, 0))
            return carry

        lax.fori_loop(0, turns, step, 0)

        @pl.when(odd == 1)
        def _():
            gather([stop - 1], turns % 2, turns - 1)
            finish([stop - 1], turns % 2)

        @pl.when(odd == 0)
        def _():
            finish(pair(turns - 1), (turns + 1) % 2)

    pairs = out_rows * 3 * len(spec)
    specs = [whole()] * len(inputs)
    scratch = []
    if stage == 0:
        scratch = [pltpu.VMEM(array.shape, array.dtype) for array in extra]
        scratch.append(pltpu.SemaphoreType.DMA((len(extra),)))
        specs[len(inputs) - len(extra) :] = [pl.BlockSpec(memory_space=pltpu.HBM)] * len(extra)
    if stage == 2:
        scratch = [pltpu.VMEM((2, 2 * features, wide), jnp.bfloat16)]
    return pl.pallas_call(
        body,
        out_shape=tuple(outs),
        in_specs=[scalars(), scalars()] + specs,
        out_specs=tuple(whole() for _ in outs),
        scratch_shapes=scratch,
        cost_estimate=pl.CostEstimate(
            flops=pairs * 2 * slots * slots * (2 * features + HEAD),
            transcendentals=pairs * 2 * slots * slots,
            bytes_accessed=pairs * 4 * slots * slots,
        ),
        compiler_params=params(),
    )(ints, flts, *inputs)


def local(
    features,
    positions,
    counts,
    old_cuts,
    new_cuts,
    radial_rates,
    conv_weight,
    up_weight,
    up_bias,
    down_weight,
    down_bias,
):
    peers = lax.axis_size("gx")
    slot_rows = features.shape[0]
    total = peers * slot_rows // 2
    most = min(slot_rows, total - 2 * (peers - 1))
    packed, edge, ints, flts = pack(
        features, positions, counts, old_cuts, new_cuts, radial_rates, most
    )

    if peers == 2:
        other = lax.ppermute(edge, "gx", [(0, 1), (1, 0)])
        frame = assemble(ints, packed, other, total)
        mid_rows = total - 1
    else:
        column = lax.axis_index("gx")
        old_low = old_cuts[column]
        old_high = old_cuts[column + 1]
        held = old_high - old_low
        frame_rows = slot_rows + 4
        base = new_cuts[column] - 2
        pieces = [packed]
        starts = [old_low]
        for by, rows in ((1, REACH), (2, 1)):
            tail_at = jnp.maximum(held - rows, 0)
            tail = lax.dynamic_slice_in_dim(packed, tail_at, rows, 0)
            pieces.append(shift(tail, "gx", by))
            back = jnp.maximum(column - by, 0)
            starts.append(jnp.maximum(old_cuts[back], old_cuts[back + 1] - rows))
            pieces.append(shift(packed[:rows], "gx", -by))
            starts.append(old_cuts[jnp.minimum(column + by, peers - 1)])
        layer = base + jnp.arange(frame_rows, dtype=jnp.int32)
        before = old_cuts[jnp.maximum(column - 1, 0)]
        after = old_cuts[jnp.minimum(column + 1, peers - 1) + 1]
        at = []
        first = 0
        for piece, begin in zip(pieces, starts):
            at.append(first + layer - begin)
            first += piece.shape[0]
        choice = jnp.where(
            layer >= old_high,
            jnp.where(layer >= after, at[4], at[2]),
            jnp.where(layer >= old_low, at[0], jnp.where(layer >= before, at[1], at[3])),
        )
        frame = jnp.take(jnp.concatenate(pieces, axis=0), jnp.clip(choice, 0, first - 1), axis=0)
        mid_rows = slot_rows + 2

    own = [(0, None, 0, 0, ())]
    sides = [
        (0, None, -1, 0, (FAR_Y,)),
        (1, None, 1, 0, ()),
        (2, 0, 0, 1, ()),
        (2, 1, -1, 1, (FAR_Y,)),
        (2, 2, 1, 1, ()),
        (3, None, 0, -1, (FAR_Z,)),
    ]
    cross = [
        (0, 0, -1, -1, (FAR_Y, FAR_Z)),
        (0, 1, 1, -1, (FAR_Z,)),
    ]
    up_turned = jnp.transpose(up_weight, (0, 2, 1))

    def layer_of(level, block, known, out_rows):
        up = whole_swap(block, other_y)
        down = partner(block, "gy")
        beyond = whole_swap(block, other_z)
        right, near0, near1, near2 = known
        made = gather_call(
            0,
            level,
            ints,
            flts,
            own,
            frame,
            [block],
            right,
            near0,
            None,
            [outside(array) for array in (up_turned, up_bias, down_bias, conv_weight)],
            out_rows,
        )
        acc, made = made[0], list(made[1:])
        if level == 0:
            right, near0 = made[:2]
        ready = made[-4:]
        acc, up, down, beyond = lax.optimization_barrier((acc, up, down, beyond))
        trio, rims = stacked(block, up, down)
        close = partner(trio, "gz")
        far = whole_swap(rims, other_z)
        made = gather_call(
            1, level, ints, flts, sides, frame, [up, down, close, beyond], right, near1, acc, [], out_rows
        )
        acc = made[0]
        if level == 0:
            near1 = made[1]
        made = gather_call(
            2,
            level,
            ints,
            flts,
            cross,
            frame,
            [far],
            right,
            near2,
            acc,
            [block, down_weight] + ready,
            out_rows,
        )
        if level == 0:
            near2 = made[1]
        return made[0], (right, near0, near1, near2)

    mid, known = layer_of(0, frame, (None,) * 4, mid_rows)
    moved, _ = layer_of(1, mid, known, slot_rows)
    return moved[:, None, None]


def solution(mesh):
    placed = (P("gx", "gy", "gz", None, None),) * 2 + (P("gx", "gy", "gz"),) + (P(),) * 8
    return jax.shard_map(
        local,
        mesh=mesh,
        in_specs=placed,
        out_specs=P("gx", "gy", "gz", None, None),
        check_vma=False,
    )
```
